32 devices in a mesh: groups: 2 (over y), probe: 4 (over z), depth: 2 (over x), tile: 2 (over core).
Axes of the slice: x: 2, y: 2, z: 4, core: 2. Of those that a mesh axis runs over, the one named last changes fastest.
Arguments:
- stored_waves: bfloat16 [2, 16, 2, 256, 256], P('depth', ('groups', 'probe', 'tile')), parts along dimension 1, may hold values from -6 to 6
- transmission: bfloat16 [2, 16, 2, 256, 256], P('depth', ('groups', 'probe', 'tile')), parts along dimension 1
- residual: float32 [16, 2, 256, 256], P(('groups', 'probe', 'tile')), parts along dimension 0, may hold values from -0.6 to 0.6
- offsets: int32 [16, 2], P('groups'), parts along dimension 0, may hold values from 0 to 256
- slot_position: int32 [16], P(('groups', 'probe', 'tile')), parts along dimension 0, may hold values from 0 to 7, each once
Outputs:
- object_gradient: float32 [4, 2, 512, 512], P('groups', 'depth', 'probe', 'tile'), parts along dimension 0
The draws below stay inside these ranges and needn't reach their ends.
There are 2 independent parts, one for each index of `groups`. The reference program is written for one: setup_inputs(seed, part) draws one part's arguments, and reference() takes and returns one part's arrays. A program takes and returns all parts, laid end to end along the dimension named above; each array names one. Nothing has to cross between parts.
Inputs may be any that keep to these rules, and one draw needn't show every extreme that they name: `slot_position`: every scan position is held by exactly one slot.
All inputs are finite; a program needn't handle non-finite values.
Results may differ from the reference program's by a relative error of at most 0.0032.
Values may be sent and summed in bfloat16 or wider, within the bound.
A program may use at most 64 MiB of HBM per device.

```python
import math
import jax
import jax.numpy as jnp
from jax import lax

W = 256
OBJ = 512
SLICES = 2
POSITIONS = 8


def draw_transmission(key, part):
    amp_key, phase_key = jax.random.split(key)
    draw_shape = (SLICES, POSITIONS, 1, W, W)
    amplitude = jnp.exp(jax.random.uniform(amp_key, draw_shape, jnp.float32, math.log(0.75), 0.0))
    phase_angle = jax.random.uniform(phase_key, draw_shape, jnp.float32, -math.pi, math.pi)
    return jnp.concatenate([amplitude * jnp.cos(phase_angle), amplitude * jnp.sin(phase_angle)], axis=2).astype(jnp.bfloat16)


def set_ends(values, own_key, least, largest):
    place = [jax.random.randint(jax.random.fold_in(own_key, axis), (), 0, length) for axis, length in enumerate(values.shape)]
    main_axis = values.shape.index(max(values.shape))
    next_to = place[:main_axis] + [(place[main_axis] + 1) % values.shape[main_axis]] + place[main_axis + 1:]
    return values.at[tuple(place)].set(least).at[tuple(next_to)].set(largest)


def block_scale(stream_key, dims, cuts, smallest, top_value):
    def one(axis_at, shards_of):
        draws = jax.random.uniform(jax.random.fold_in(jax.random.fold_in(stream_key, 6), axis_at), (shards_of,), jnp.float32, smallest / len(cuts), top_value / len(cuts))
        return jnp.repeat(jnp.exp(draws), dims[axis_at] // shards_of).reshape((-1,) + (1,) * (len(dims) - axis_at - 1))

    level = one(*cuts[0])
    for cut in cuts[1:]:
        level = level * one(*cut)
    return level


def centred(rng, shape, scale, reach, cuts=(), kind=jnp.bfloat16):
    values = jax.random.normal(rng, shape, jnp.float32) * scale
    if len(cuts) > 0:
        values = block_scale(rng, shape, cuts, -0.22, 0.18) * values
    return jnp.clip(values, min=-reach, max=reach).astype(kind)


def setup_inputs(seed: int = 0, part: int = 0) -> dict:
    keys = jax.random.split(jax.random.key(seed), 6)
    own_keys = jax.random.split(jax.random.fold_in(keys[5], part), 6)
    stored_waves = centred(own_keys[0], (SLICES, POSITIONS, 2, W, W), 1.0, 6.0, ((0, 2), (1, 8)))
    transmission = draw_transmission(jax.random.fold_in(jax.random.fold_in(keys[5], part), 71), part)
    residual = centred(own_keys[2], (POSITIONS, 2, W, W), 0.1, 0.6, ((0, 8),), jnp.float32)
    offsets = set_ends(jax.random.randint(own_keys[3], (POSITIONS, 2), 0, OBJ - W + 1), jax.random.fold_in(own_keys[3], 1), 0, OBJ - W).astype(jnp.int32)
    slot_position = jax.random.permutation(own_keys[4], POSITIONS).astype(jnp.int32)
    return dict(stored_waves=stored_waves, transmission=transmission, residual=residual, offsets=offsets, slot_position=slot_position)


def back_propagate(field_real, field_imag):
    side_length = field_real.shape[-1]
    counter = jnp.arange(side_length, dtype=jnp.int32)
    frequency = ((counter + side_length // 2) % side_length - side_length // 2).astype(jnp.float32)
    phase_angle = 0.5 * (frequency[:, None] * frequency[:, None] + frequency[None, :] * frequency[None, :]) / side_length
    spectrum = jnp.fft.fft2(field_real + 1j * field_imag)
    spectrum = spectrum * (jnp.cos(phase_angle) + 1j * jnp.sin(phase_angle))
    result = jnp.fft.ifft2(spectrum)
    return jnp.real(result), jnp.imag(result)


def reference(stored_waves, transmission, residual, offsets, slot_position):
    slice_count = stored_waves.shape[0]
    positions = stored_waves.shape[1]
    side_length = stored_waves.shape[-1]
    corners = offsets[slot_position]
    adjoint_real = residual[:, 0]
    adjoint_imag = residual[:, 1]
    handed_real = adjoint_real
    handed_imag = adjoint_imag
    grads_real = []
    grads_imag = []
    for slice_number in range(slice_count - 1, -1, -1):
        if slice_number < slice_count - 1:
            adjoint_real, adjoint_imag = back_propagate(handed_real, handed_imag)
        wave_real = stored_waves[slice_number, :, 0].astype(jnp.float32)
        wave_imag = stored_waves[slice_number, :, 1].astype(jnp.float32)
        grads_real.insert(0, wave_real * adjoint_real + wave_imag * adjoint_imag)
        grads_imag.insert(0, wave_real * adjoint_imag - wave_imag * adjoint_real)
        trans_real = transmission[slice_number, :, 0].astype(jnp.float32)
        trans_imag = transmission[slice_number, :, 1].astype(jnp.float32)
        rounded = lax.optimization_barrier(((trans_real * adjoint_real + trans_imag * adjoint_imag).astype(jnp.bfloat16),
                                            (trans_real * adjoint_imag - trans_imag * adjoint_real).astype(jnp.bfloat16)))
        handed_real = rounded[0].astype(jnp.float32)
        handed_imag = rounded[1].astype(jnp.float32)
    gradient = jnp.stack([jnp.stack(grads_real), jnp.stack(grads_imag)])
    region = jnp.zeros((2, slice_count, OBJ, OBJ), jnp.float32)

    def add_patch(number, region):
        patch_value = lax.dynamic_index_in_dim(gradient, number, 2, keepdims=False)
        anchor = jnp.int32(0)
        corner = (anchor, anchor, corners[number, 0].astype(jnp.int32), corners[number, 1].astype(jnp.int32))
        current = lax.dynamic_slice(region, corner, (2, slice_count, side_length, side_length))
        return lax.dynamic_update_slice(region, current + patch_value, corner)

    return lax.fori_loop(0, positions, add_patch, region)
```

```python
import functools

import jax
import jax.numpy as jnp
import ml_dtypes
import numpy as np
from jax import lax
from jax.experimental import pallas as pl
from jax.experimental.pallas import tpu as pltpu
from jax.sharding import PartitionSpec as P

OBJ = 512
CHUNKS = 4
MESH = pl.DeviceIdType.MESH
F32 = jnp.float32
BF16 = jnp.bfloat16


def propagator(side):
    counter = np.arange(side)
    frequency = (counter + side // 2) % side - side // 2
    chirp = np.exp(0.5j * frequency.astype(np.float64) ** 2 / side)
    column = np.fft.ifft(chirp)
    matrix = column[(counter[:, None] - counter[None, :]) % side]
    parts = np.stack([matrix.real, matrix.imag])
    high = parts.astype(ml_dtypes.bfloat16)
    low = (parts - high.astype(np.float64)).astype(ml_dtypes.bfloat16)
    return high, low


def dot(a, b):
    return jnp.dot(a, b, preferred_element_type=F32)


def split(value):
    high = value.astype(BF16)
    return high, (value - high.astype(F32)).astype(BF16)


def conj_times(layer_real, layer_imag, real, imag):
    return (
        layer_real * real + layer_imag * imag,
        layer_real * imag - layer_imag * real,
    )


def flip(index, mask, count):
    result, bit = 0, 1
    while bit < count:
        result = result + ((index // bit + (mask // bit) % 2) % 2) * bit
        bit *= 2
    return result


def kernel(
    depth_count,
    probe_count,
    waves,
    layers,
    residual,
    offsets,
    slot,
    high,
    low,
    out,
    hand_out,
    hand_in,
    turned_high,
    turned_low,
    grads,
    corners,
    strips_out,
    strips_in,
    hand_sems,
    grad_sems,
    corner_sems,
    strip_sems,
):
    side = waves.shape[-1]
    rows, columns = out.shape[2], out.shape[3]
    step = side // CHUNKS
    depth = lax.axis_index("depth")
    probe = lax.axis_index("probe")
    tile = lax.axis_index("tile")
    is_top = depth == depth_count - 1
    has_below = depth > 0

    barrier = pltpu.get_barrier_semaphore()
    for mask in range(1, probe_count):
        pl.semaphore_signal(
            barrier, inc=1, device_id={"probe": flip(probe, mask, probe_count)}, device_id_type=MESH
        )
    pl.semaphore_signal(barrier, inc=1, device_id={"tile": 1 - tile}, device_id_type=MESH)

    @pl.when(depth < depth_count - 1)
    def _():
        pl.semaphore_signal(barrier, inc=1, device_id={"depth": depth + 1}, device_id_type=MESH)

    own_slot = slot[0]
    top_row = offsets[own_slot, 0]
    left_column = offsets[own_slot, 1]
    corners[0, 0:8, :] = jnp.full((8, side), top_row, jnp.int32)
    corners[0, 8:16, :] = jnp.full((8, side), left_column, jnp.int32)

    @pl.when(has_below)
    def _():
        pl.semaphore_wait(barrier, probe_count + 1)

    @pl.when(jnp.logical_not(has_below))
    def _():
        pl.semaphore_wait(barrier, probe_count)

    corner_copy = pltpu.make_async_remote_copy(
        src_ref=corners.at[0],
        dst_ref=corners.at[1],
        send_sem=corner_sems.at[0],
        recv_sem=corner_sems.at[1],
        device_id={"tile": 1 - tile},
        device_id_type=MESH,
    )
    corner_copy.start()

    def hand_copy(part):
        window = pl.ds(part * step, step)
        return pltpu.make_async_remote_copy(
            src_ref=hand_out.at[:, window, :],
            dst_ref=hand_in.at[:, window, :],
            send_sem=hand_sems.at[0, part],
            recv_sem=hand_sems.at[1, part],
            device_id={"depth": depth - 1},
            device_id_type=MESH,
        )

    def grad_copy(part):
        window = pl.ds(part * step, step)
        return pltpu.make_async_remote_copy(
            src_ref=grads.at[0, :, window, :],
            dst_ref=grads.at[1, :, window, :],
            send_sem=grad_sems.at[0, part],
            recv_sem=grad_sems.at[1, part],
            device_id={"tile": 1 - tile},
            device_id_type=MESH,
        )

    def hand_down(part, real, imag):
        window = pl.ds(part * step, step)
        handed = conj_times(
            layers[0, 0, 0, window, :].astype(F32), layers[0, 0, 1, window, :].astype(F32), real, imag
        )
        hand_out[0, window, :] = handed[0].astype(BF16)
        hand_out[1, window, :] = handed[1].astype(BF16)
        hand_copy(part).start()

    def give_gradient(part, real, imag):
        window = pl.ds(part * step, step)
        gradient = conj_times(
            waves[0, 0, 0, window, :].astype(F32), waves[0, 0, 1, window, :].astype(F32), real, imag
        )
        grads[0, 0, window, :] = gradient[0].astype(BF16)
        grads[0, 1, window, :] = gradient[1].astype(BF16)
        grad_copy(part).start()

    @pl.when(is_top)
    def _():
        if depth_count > 1:
            for part in range(CHUNKS):
                window = pl.ds(part * step, step)
                hand_down(part, residual[0, 0, window, :], residual[0, 1, window, :])
        for part in range(CHUNKS):
            window = pl.ds(part * step, step)
            give_gradient(part, residual[0, 0, window, :], residual[0, 1, window, :])

    if depth_count > 1:

        @pl.when(depth < depth_count - 1)
        def _():
            for part in range(CHUNKS):
                window = pl.ds(part * step, step)
                hand_copy(part).wait_recv()
                real, imag = hand_in[0, window, :], hand_in[1, window, :]

                def times(index):
                    return (
                        dot(real, high[index]) + dot(real, low[index]),
                        dot(imag, high[index]) + dot(imag, low[index]),
                    )

                real_cos, imag_cos = times(0)
                real_sin, imag_sin = times(1)
                for index, value in enumerate((real_cos - imag_sin, real_sin + imag_cos)):
                    turned_high[index, window, :], turned_low[index, window, :] = split(value)

            for part in range(CHUNKS):
                window = pl.ds(part * step, step)

                def from_left(table, field):
                    return (
                        dot(high[table, window, :], turned_high[field])
                        + dot(low[table, window, :], turned_high[field])
                        + dot(high[table, window, :], turned_low[field])
                    )

                real = from_left(0, 0) - from_left(1, 1)
                imag = from_left(0, 1) + from_left(1, 0)
                if depth_count > 2:

                    @pl.when(has_below)
                    def _():
                        hand_down(part, real, imag)

                give_gradient(part, real, imag)

    row_index = lax.broadcasted_iota(jnp.int32, (side, columns), 0)
    column_index = lax.broadcasted_iota(jnp.int32, (side, columns), 1) + tile * columns

    def onehot(match):
        return jnp.where(match, 1.0, 0.0).astype(BF16)

    own_columns = onehot(column_index - row_index == left_column)
    placed = [[dot(grads[0, c], own_columns).astype(BF16)] for c in range(2)]

    corner_copy.wait_recv()
    for part in range(CHUNKS):
        grad_copy(part).wait_recv()
    peer_row = corners[1, 0:1, :]
    peer_columns = onehot(column_index - row_index == corners[1, 8:9, 0:columns])
    for c in range(2):
        placed[c].append(dot(grads[1, c], peer_columns).astype(BF16))

    strip_row = lax.broadcasted_iota(jnp.int32, (rows, side), 0)
    patch_row = lax.broadcasted_iota(jnp.int32, (rows, side), 1)
    distance = strip_row - patch_row

    def strip(owner):
        shifted = distance + owner * rows
        own_rows = onehot(shifted == top_row)
        peer_rows = onehot(shifted == peer_row)
        return [dot(own_rows, placed[c][0]) + dot(peer_rows, placed[c][1]) for c in range(2)]

    def strip_copy(mask):
        return pltpu.make_async_remote_copy(
            src_ref=strips_out.at[mask - 1],
            dst_ref=strips_in.at[mask - 1],
            send_sem=strip_sems.at[0, mask - 1],
            recv_sem=strip_sems.at[1, mask - 1],
            device_id={"probe": flip(probe, mask, probe_count)},
            device_id_type=MESH,
        )

    for mask in range(probe_count - 1, 0, -1):
        real, imag = strip(flip(probe, mask, probe_count))
        strips_out[mask - 1, 0] = real.astype(BF16)
        strips_out[mask - 1, 1] = imag.astype(BF16)
        strip_copy(mask).start()
    total = strip(probe)
    for c in range(2):
        out[c, 0] = total[c]
    for mask in range(1, probe_count):
        strip_copy(mask).wait_recv()
        for c in range(2):
            out[c, 0] += strips_in[mask - 1, c].astype(F32)

    corner_copy.wait_send()
    for part in range(CHUNKS):
        grad_copy(part).wait_send()
    for mask in range(1, probe_count):
        strip_copy(mask).wait_send()

    @pl.when(has_below)
    def _():
        for part in range(CHUNKS):
            hand_copy(part).wait_send()


def per_device(depth_count, probe_count, tile_count, waves, layers, residual, offsets, slot):
    side = waves.shape[-1]
    high, low = propagator(side)
    rows, columns = OBJ // probe_count, OBJ // tile_count
    vmem = pl.BlockSpec(memory_space=pltpu.VMEM)
    smem = pl.BlockSpec(memory_space=pltpu.SMEM)
    return pl.pallas_call(
        functools.partial(kernel, depth_count, probe_count),
        out_shape=jax.ShapeDtypeStruct((2, 1, rows, columns), F32),
        in_specs=[vmem, vmem, vmem, smem, smem, vmem, vmem],
        out_specs=vmem,
        scratch_shapes=[
            pltpu.VMEM((2, side, side), BF16),
            pltpu.VMEM((2, side, side), BF16),
            pltpu.VMEM((2, side, side), BF16),
            pltpu.VMEM((2, side, side), BF16),
            pltpu.VMEM((2, 2, side, side), BF16),
            pltpu.VMEM((2, 16, side), jnp.int32),
            pltpu.VMEM((probe_count - 1, 2, rows, columns), BF16),
            pltpu.VMEM((probe_count - 1, 2, rows, columns), BF16),
            pltpu.SemaphoreType.DMA((2, CHUNKS)),
            pltpu.SemaphoreType.DMA((2, CHUNKS)),
            pltpu.SemaphoreType.DMA((2,)),
            pltpu.SemaphoreType.DMA((2, probe_count - 1)),
        ],
        compiler_params=pltpu.CompilerParams(
            collective_id=0, has_side_effects=True, vmem_limit_bytes=32 * 1024 * 1024
        ),
    )(waves, layers, residual, offsets, slot, jnp.asarray(high), jnp.asarray(low))


def solution(mesh):
    return jax.shard_map(
        functools.partial(per_device, mesh.shape["depth"], mesh.shape["probe"], mesh.shape["tile"]),
        mesh=mesh,
        in_specs=(
            P("depth", ("groups", "probe", "tile"), None, None, None),
            P("depth", ("groups", "probe", "tile"), None, None, None),
            P(("groups", "probe", "tile"), None, None, None),
            P("groups", None),
            P(("groups", "probe", "tile")),
        ),
        out_specs=P("groups", "depth", "probe", "tile"),
        check_vma=False,
    )
```

```python
import functools

import jax
import jax.numpy as jnp
import ml_dtypes
import numpy as np
from jax import lax
from jax.experimental import pallas as pl
from jax.experimental.pallas import tpu as pltpu
from jax.sharding import PartitionSpec as P

OBJ = 512
CHUNKS = 4
MESH = pl.DeviceIdType.MESH
F32 = jnp.float32
BF16 = jnp.bfloat16


def propagator(side):
    counter = np.arange(side)
    frequency = (counter + side // 2) % side - side // 2
    chirp = np.exp(0.5j * frequency.astype(np.float64) ** 2 / side)
    column = np.fft.ifft(chirp)
    matrix = column[(counter[:, None] - counter[None, :]) % side]
    parts = np.concatenate([matrix.real, matrix.imag], axis=1)
    high = parts.astype(ml_dtypes.bfloat16)
    low = (parts - high.astype(np.float64)).astype(ml_dtypes.bfloat16)
    return np.stack([high, low])


def dot(a, b):
    return jnp.dot(a, b, preferred_element_type=F32)


def split(value):
    high = value.astype(BF16)
    return high, (value - high.astype(F32)).astype(BF16)


def conj_times(layer_real, layer_imag, real, imag):
    return (
        layer_real * real + layer_imag * imag,
        layer_real * imag - layer_imag * real,
    )


def flip(index, mask, count):
    result, bit = 0, 1
    while bit < count:
        result = result + ((index // bit + (mask // bit) % 2) % 2) * bit
        bit *= 2
    return result


def kernel(
    depth_count,
    probe_count,
    waves_hbm,
    layers_hbm,
    residual_hbm,
    offsets,
    slot,
    table_hbm,
    out,
    waves,
    layers,
    residual,
    table,
    hand_out,
    hand_in,
    turned,
    grads,
    corners,
    strips_out,
    strips_in,
    load_sems,
    hand_sems,
    grad_sems,
    corner_sems,
    strip_sems,
):
    side = waves.shape[-1]
    rows, columns = out.shape[2], out.shape[3]
    step = side // CHUNKS
    depth = lax.axis_index("depth")
    probe = lax.axis_index("probe")
    tile = lax.axis_index("tile")
    is_top = depth == depth_count - 1
    has_below = depth > 0

    barrier = pltpu.get_barrier_semaphore()
    for mask in range(1, probe_count):
        pl.semaphore_signal(
            barrier, inc=1, device_id={"probe": flip(probe, mask, probe_count)}, device_id_type=MESH
        )
    pl.semaphore_signal(barrier, inc=1, device_id={"tile": 1 - tile}, device_id_type=MESH)

    @pl.when(depth < depth_count - 1)
    def _():
        pl.semaphore_signal(barrier, inc=1, device_id={"depth": depth + 1}, device_id_type=MESH)

    load_residual = pltpu.make_async_copy(residual_hbm, residual, load_sems.at[0])
    load_layers = pltpu.make_async_copy(layers_hbm, layers, load_sems.at[1])
    load_waves = pltpu.make_async_copy(waves_hbm, waves, load_sems.at[2])
    load_table = pltpu.make_async_copy(table_hbm, table, load_sems.at[3])

    @pl.when(is_top)
    def _():
        load_residual.start()

    if depth_count > 1:

        @pl.when(has_below)
        def _():
            load_layers.start()

        @pl.when(jnp.logical_not(is_top))
        def _():
            load_table.start()

    load_waves.start()

    own_slot = slot[0]
    top_row = offsets[own_slot, 0]
    left_column = offsets[own_slot, 1]
    corners[0, 0:8, :] = jnp.full((8, side), top_row, jnp.int32)
    corners[0, 8:16, :] = jnp.full((8, side), left_column, jnp.int32)

    @pl.when(has_below)
    def _():
        pl.semaphore_wait(barrier, probe_count + 1)

    @pl.when(jnp.logical_not(has_below))
    def _():
        pl.semaphore_wait(barrier, probe_count)

    corner_copy = pltpu.make_async_remote_copy(
        src_ref=corners.at[0],
        dst_ref=corners.at[1],
        send_sem=corner_sems.at[0],
        recv_sem=corner_sems.at[1],
        device_id={"tile": 1 - tile},
        device_id_type=MESH,
    )
    corner_copy.start()

    def hand_copy(part):
        window = pl.ds(part * step, step)
        return pltpu.make_async_remote_copy(
            src_ref=hand_out.at[:, window, :],
            dst_ref=hand_in.at[:, window, :],
            send_sem=hand_sems.at[0, part],
            recv_sem=hand_sems.at[1, part],
            device_id={"depth": depth - 1},
            device_id_type=MESH,
        )

    def grad_copy(part):
        window = pl.ds(part * step, step)
        return pltpu.make_async_remote_copy(
            src_ref=grads.at[0, :, window, :],
            dst_ref=grads.at[1, :, window, :],
            send_sem=grad_sems.at[0, part],
            recv_sem=grad_sems.at[1, part],
            device_id={"tile": 1 - tile},
            device_id_type=MESH,
        )

    def hand_down(part, real, imag):
        window = pl.ds(part * step, step)
        handed = conj_times(
            layers[0, 0, 0, window, :].astype(F32), layers[0, 0, 1, window, :].astype(F32), real, imag
        )
        hand_out[0, window, :] = handed[0].astype(BF16)
        hand_out[1, window, :] = handed[1].astype(BF16)
        hand_copy(part).start()

    def give_gradient(part, real, imag):
        window = pl.ds(part * step, step)
        gradient = conj_times(
            waves[0, 0, 0, window, :].astype(F32), waves[0, 0, 1, window, :].astype(F32), real, imag
        )
        grads[0, 0, window, :] = gradient[0].astype(BF16)
        grads[0, 1, window, :] = gradient[1].astype(BF16)
        grad_copy(part).start()

    @pl.when(is_top)
    def _():
        load_residual.wait()
        if depth_count > 1:
            load_layers.wait()
            for part in range(CHUNKS):
                window = pl.ds(part * step, step)
                hand_down(part, residual[0, 0, window, :], residual[0, 1, window, :])
        load_waves.wait()
        for part in range(CHUNKS):
            window = pl.ds(part * step, step)
            give_gradient(part, residual[0, 0, window, :], residual[0, 1, window, :])

    if depth_count > 1:

        @pl.when(jnp.logical_not(is_top))
        def _():
            load_table.wait()
            load_waves.wait()
            if depth_count > 2:

                @pl.when(has_below)
                def _():
                    load_layers.wait()

            for part in range(CHUNKS):
                window = pl.ds(part * step, step)
                hand_copy(part).wait_recv()
                real = dot(hand_in[0, window, :], table[0]) + dot(hand_in[0, window, :], table[1])
                imag = dot(hand_in[1, window, :], table[0]) + dot(hand_in[1, window, :], table[1])
                product = real[:, :side] - imag[:, side:], real[:, side:] + imag[:, :side]
                for c in range(2):
                    top, rest = split(product[c])
                    turned[0, window, pl.ds(c * side, side)] = top
                    turned[1, window, pl.ds(c * side, side)] = rest

            for part in range(CHUNKS):
                window = pl.ds(part * step, step)

                def from_left(index):
                    columns = pl.ds(index * side, side)
                    return (
                        dot(table[0, window, columns], turned[0])
                        + dot(table[1, window, columns], turned[0])
                        + dot(table[0, window, columns], turned[1])
                    )

                by_real, by_imag = from_left(0), from_left(1)
                real = by_real[:, :side] - by_imag[:, side:]
                imag = by_real[:, side:] + by_imag[:, :side]
                if depth_count > 2:

                    @pl.when(has_below)
                    def _():
                        hand_down(part, real, imag)

                give_gradient(part, real, imag)

    row_index = lax.broadcasted_iota(jnp.int32, (side, columns), 0)
    column_index = lax.broadcasted_iota(jnp.int32, (side, columns), 1) + tile * columns

    def onehot(match):
        return jnp.where(match, 1.0, 0.0).astype(BF16)

    own_columns = onehot(column_index - row_index == left_column)
    placed = [[dot(grads[0, c], own_columns).astype(BF16)] for c in range(2)]

    corner_copy.wait_recv()
    for part in range(CHUNKS):
        grad_copy(part).wait_recv()
    peer_row = corners[1, 0:1, :]
    peer_columns = onehot(column_index - row_index == corners[1, 8:9, 0:columns])
    for c in range(2):
        placed[c].append(dot(grads[1, c], peer_columns).astype(BF16))

    strip_row = lax.broadcasted_iota(jnp.int32, (rows, side), 0)
    patch_row = lax.broadcasted_iota(jnp.int32, (rows, side), 1)
    distance = strip_row - patch_row

    def strip(owner):
        shifted = distance + owner * rows
        own_rows = onehot(shifted == top_row)
        peer_rows = onehot(shifted == peer_row)
        return [dot(own_rows, placed[c][0]) + dot(peer_rows, placed[c][1]) for c in range(2)]

    def strip_copy(mask):
        return pltpu.make_async_remote_copy(
            src_ref=strips_out.at[mask - 1],
            dst_ref=strips_in.at[mask - 1],
            send_sem=strip_sems.at[0, mask - 1],
            recv_sem=strip_sems.at[1, mask - 1],
            device_id={"probe": flip(probe, mask, probe_count)},
            device_id_type=MESH,
        )

    for mask in range(probe_count - 1, 0, -1):
        real, imag = strip(flip(probe, mask, probe_count))
        strips_out[mask - 1, 0] = real.astype(BF16)
        strips_out[mask - 1, 1] = imag.astype(BF16)
        strip_copy(mask).start()
    total = strip(probe)
    for c in range(2):
        out[c, 0] = total[c]
    for mask in range(1, probe_count):
        strip_copy(mask).wait_recv()
        for c in range(2):
            out[c, 0] += strips_in[mask - 1, c].astype(F32)

    corner_copy.wait_send()
    for part in range(CHUNKS):
        grad_copy(part).wait_send()
    for mask in range(1, probe_count):
        strip_copy(mask).wait_send()

    @pl.when(has_below)
    def _():
        for part in range(CHUNKS):
            hand_copy(part).wait_send()


def per_device(depth_count, probe_count, tile_count, waves, layers, residual, offsets, slot):
    side = waves.shape[-1]
    table = propagator(side)
    rows, columns = OBJ // probe_count, OBJ // tile_count
    vmem = pl.BlockSpec(memory_space=pltpu.VMEM)
    smem = pl.BlockSpec(memory_space=pltpu.SMEM)
    hbm = pl.BlockSpec(memory_space=pltpu.HBM)
    return pl.pallas_call(
        functools.partial(kernel, depth_count, probe_count),
        out_shape=jax.ShapeDtypeStruct((2, 1, rows, columns), F32),
        in_specs=[hbm, hbm, hbm, smem, smem, hbm],
        out_specs=vmem,
        scratch_shapes=[
            pltpu.VMEM(waves.shape, waves.dtype),
            pltpu.VMEM(layers.shape, layers.dtype),
            pltpu.VMEM(residual.shape, residual.dtype),
            pltpu.VMEM(table.shape, BF16),
            pltpu.VMEM((2, side, side), BF16),
            pltpu.VMEM((2, side, side), BF16),
            pltpu.VMEM((2, side, 2 * side), BF16),
            pltpu.VMEM((2, 2, side, side), BF16),
            pltpu.VMEM((2, 16, side), jnp.int32),
            pltpu.VMEM((probe_count - 1, 2, rows, columns), BF16),
            pltpu.VMEM((probe_count - 1, 2, rows, columns), BF16),
            pltpu.SemaphoreType.DMA((4,)),
            pltpu.SemaphoreType.DMA((2, CHUNKS)),
            pltpu.SemaphoreType.DMA((2, CHUNKS)),
            pltpu.SemaphoreType.DMA((2,)),
            pltpu.SemaphoreType.DMA((2, probe_count - 1)),
        ],
        compiler_params=pltpu.CompilerParams(
            collective_id=0, has_side_effects=True, vmem_limit_bytes=32 * 1024 * 1024
        ),
    )(waves, layers, residual, offsets, slot, jnp.asarray(table))


def solution(mesh):
    return jax.shard_map(
        functools.partial(per_device, mesh.shape["depth"], mesh.shape["probe"], mesh.shape["tile"]),
        mesh=mesh,
        in_specs=(
            P("depth", ("groups", "probe", "tile"), None, None, None),
            P("depth", ("groups", "probe", "tile"), None, None, None),
            P(("groups", "probe", "tile"), None, None, None),
            P("groups", None),
            P(("groups", "probe", "tile")),
        ),
        out_specs=P("groups", "depth", "probe", "tile"),
        check_vma=False,
    )
```

```python
import functools

import jax
import jax.numpy as jnp
import ml_dtypes
import numpy as np
from jax import lax
from jax.experimental import pallas as pl
from jax.experimental.pallas import tpu as pltpu
from jax.sharding import PartitionSpec as P

OBJ = 512
CHUNKS = 4
MESH = pl.DeviceIdType.MESH
F32 = jnp.float32
BF16 = jnp.bfloat16


def propagator(side):
    counter = np.arange(side)
    frequency = (counter + side // 2) % side - side // 2
    chirp = np.exp(0.5j * frequency.astype(np.float64) ** 2 / side)
    column = np.fft.ifft(chirp)
    matrix = column[(counter[:, None] - counter[None, :]) % side]
    parts = np.concatenate([matrix.real, matrix.imag], axis=1)
    high = parts.astype(ml_dtypes.bfloat16)
    low = (parts - high.astype(np.float64)).astype(ml_dtypes.bfloat16)
    return np.stack([high, low])


def dot(a, b):
    return jnp.dot(a, b, preferred_element_type=F32)


def split(value):
    high = value.astype(BF16)
    return high, (value - high.astype(F32)).astype(BF16)


def conj_times(layer_real, layer_imag, real, imag):
    return (
        layer_real * real + layer_imag * imag,
        layer_real * imag - layer_imag * real,
    )


def flip(index, mask, count):
    result, bit = 0, 1
    while bit < count:
        result = result + ((index // bit + (mask // bit) % 2) % 2) * bit
        bit *= 2
    return result


def kernel(
    depth_count,
    probe_count,
    waves_hbm,
    layers_hbm,
    residual_hbm,
    offsets,
    slot,
    table_hbm,
    out,
    waves,
    layers,
    residual,
    table,
    hand_out,
    hand_in,
    turned,
    grads,
    corners,
    strips_out,
    strips_in,
    load_sems,
    hand_sems,
    grad_sems,
    corner_sems,
    strip_sems,
):
    side = waves.shape[-1]
    rows, columns = out.shape[2], out.shape[3]
    step = side // CHUNKS
    depth = lax.axis_index("depth")
    probe = lax.axis_index("probe")
    tile = lax.axis_index("tile")
    is_top = depth == depth_count - 1
    has_below = depth > 0

    barrier = pltpu.get_barrier_semaphore()
    for mask in range(1, probe_count):
        pl.semaphore_signal(
            barrier, inc=1, device_id={"probe": flip(probe, mask, probe_count)}, device_id_type=MESH
        )
    pl.semaphore_signal(barrier, inc=1, device_id={"tile": 1 - tile}, device_id_type=MESH)

    @pl.when(depth < depth_count - 1)
    def _():
        pl.semaphore_signal(barrier, inc=1, device_id={"depth": depth + 1}, device_id_type=MESH)

    load_residual = pltpu.make_async_copy(residual_hbm, residual, load_sems.at[0])
    load_layers = pltpu.make_async_copy(layers_hbm, layers, load_sems.at[1])
    load_waves = pltpu.make_async_copy(waves_hbm, waves, load_sems.at[2])
    load_table = pltpu.make_async_copy(table_hbm, table, load_sems.at[3])

    @pl.when(is_top)
    def _():
        load_residual.start()

    if depth_count > 1:

        @pl.when(has_below)
        def _():
            load_layers.start()

        @pl.when(jnp.logical_not(is_top))
        def _():
            load_table.start()

    load_waves.start()

    own_slot = slot[0]
    top_row = offsets[own_slot, 0]
    left_column = offsets[own_slot, 1]
    corners[0, 0:8, :] = jnp.full((8, side), top_row, jnp.int32)
    corners[0, 8:16, :] = jnp.full((8, side), left_column, jnp.int32)

    @pl.when(has_below)
    def _():
        pl.semaphore_wait(barrier, probe_count + 1)

    @pl.when(jnp.logical_not(has_below))
    def _():
        pl.semaphore_wait(barrier, probe_count)

    corner_copy = pltpu.make_async_remote_copy(
        src_ref=corners.at[0],
        dst_ref=corners.at[1],
        send_sem=corner_sems.at[0],
        recv_sem=corner_sems.at[1],
        device_id={"tile": 1 - tile},
        device_id_type=MESH,
    )
    corner_copy.start()

    def hand_copy(part):
        window = pl.ds(part * step, step)
        return pltpu.make_async_remote_copy(
            src_ref=hand_out.at[:, window, :],
            dst_ref=hand_in.at[:, window, :],
            send_sem=hand_sems.at[0, part],
            recv_sem=hand_sems.at[1, part],
            device_id={"depth": depth - 1},
            device_id_type=MESH,
        )

    def grad_copy(part):
        window = pl.ds(part * step, step)
        return pltpu.make_async_remote_copy(
            src_ref=grads.at[0, :, window, :],
            dst_ref=grads.at[1, :, window, :],
            send_sem=grad_sems.at[0, part],
            recv_sem=grad_sems.at[1, part],
            device_id={"tile": 1 - tile},
            device_id_type=MESH,
        )

    def hand_down(part, real, imag):
        window = pl.ds(part * step, step)
        handed = conj_times(
            layers[0, 0, 0, window, :].astype(F32), layers[0, 0, 1, window, :].astype(F32), real, imag
        )
        hand_out[0, window, :] = handed[0].astype(BF16)
        hand_out[1, window, :] = handed[1].astype(BF16)
        hand_copy(part).start()

    def give_gradient(part, real, imag):
        window = pl.ds(part * step, step)
        gradient = conj_times(
            waves[0, 0, 0, window, :].astype(F32), waves[0, 0, 1, window, :].astype(F32), real, imag
        )
        grads[0, 0, window, :] = gradient[0].astype(BF16)
        grads[0, 1, window, :] = gradient[1].astype(BF16)
        grad_copy(part).start()

    @pl.when(is_top)
    def _():
        load_residual.wait()
        if depth_count > 1:
            load_layers.wait()
            for part in range(CHUNKS):
                window = pl.ds(part * step, step)
                hand_down(part, residual[0, 0, window, :], residual[0, 1, window, :])
        load_waves.wait()
        for part in range(CHUNKS):
            window = pl.ds(part * step, step)
            give_gradient(part, residual[0, 0, window, :], residual[0, 1, window, :])

    if depth_count > 1:

        @pl.when(jnp.logical_not(is_top))
        def _():
            load_table.wait()
            load_waves.wait()
            if depth_count > 2:

                @pl.when(has_below)
                def _():
                    load_layers.wait()

            for part in range(CHUNKS):
                window = pl.ds(part * step, step)
                hand_copy(part).wait_recv()
                real = dot(hand_in[0, window, :], table[0]) + dot(hand_in[0, window, :], table[1])
                imag = dot(hand_in[1, window, :], table[0]) + dot(hand_in[1, window, :], table[1])
                product = real[:, :side] - imag[:, side:], real[:, side:] + imag[:, :side]
                for c in range(2):
                    top, rest = split(product[c])
                    turned[0, window, pl.ds(c * side, side)] = top
                    turned[1, window, pl.ds(c * side, side)] = rest

            for part in range(CHUNKS):
                window = pl.ds(part * step, step)

                def from_left(index):
                    columns = pl.ds(index * side, side)
                    return (
                        dot(table[0, window, columns], turned[0])
                        + dot(table[1, window, columns], turned[0])
                        + dot(table[0, window, columns], turned[1])
                    )

                by_real, by_imag = from_left(0), from_left(1)
                real = by_real[:, :side] - by_imag[:, side:]
                imag = by_real[:, side:] + by_imag[:, :side]
                if depth_count > 2:

                    @pl.when(has_below)
                    def _():
                        hand_down(part, real, imag)

                give_gradient(part, real, imag)

    row_index = lax.broadcasted_iota(jnp.int32, (side, columns), 0)
    column_index = lax.broadcasted_iota(jnp.int32, (side, columns), 1) + tile * columns

    def onehot(match):
        return jnp.where(match, 1.0, 0.0).astype(BF16)

    own_columns = onehot(column_index - row_index == left_column)
    placed = [[dot(grads[0, c], own_columns).astype(BF16)] for c in range(2)]

    corner_copy.wait_recv()
    for part in range(CHUNKS):
        grad_copy(part).wait_recv()
    peer_row = corners[1, 0:1, :]
    peer_columns = onehot(column_index - row_index == corners[1, 8:9, 0:columns])
    for c in range(2):
        placed[c].append(dot(grads[1, c], peer_columns).astype(BF16))

    strip_row = lax.broadcasted_iota(jnp.int32, (rows, side), 0)
    patch_row = lax.broadcasted_iota(jnp.int32, (rows, side), 1)
    distance = strip_row - patch_row

    def strip(owner):
        shifted = distance + owner * rows
        own_rows = onehot(shifted == top_row)
        peer_rows = onehot(shifted == peer_row)
        return [dot(own_rows, placed[c][0]) + dot(peer_rows, placed[c][1]) for c in range(2)]

    def strip_copy(mask):
        return pltpu.make_async_remote_copy(
            src_ref=strips_out.at[mask - 1],
            dst_ref=strips_in.at[mask - 1],
            send_sem=strip_sems.at[0, mask - 1],
            recv_sem=strip_sems.at[1, mask - 1],
            device_id={"probe": flip(probe, mask, probe_count)},
            device_id_type=MESH,
        )

    for mask in range(probe_count - 1, 0, -1):
        real, imag = strip(flip(probe, mask, probe_count))
        strips_out[mask - 1, 0] = real.astype(BF16)
        strips_out[mask - 1, 1] = imag.astype(BF16)
        strip_copy(mask).start()
    total = strip(probe)
    for c in range(2):
        out[c, 0] = total[c]
    for mask in range(1, probe_count):
        strip_copy(mask).wait_recv()
        for c in range(2):
            out[c, 0] += strips_in[mask - 1, c].astype(F32)

    corner_copy.wait_send()
    for part in range(CHUNKS):
        grad_copy(part).wait_send()
    for mask in range(1, probe_count):
        strip_copy(mask).wait_send()

    @pl.when(has_below)
    def _():
        for part in range(CHUNKS):
            hand_copy(part).wait_send()


def per_device(depth_count, probe_count, tile_count, waves, layers, residual, offsets, slot):
    side = waves.shape[-1]
    table = propagator(side)
    rows, columns = OBJ // probe_count, OBJ // tile_count
    vmem = pl.BlockSpec(memory_space=pltpu.VMEM)
    smem = pl.BlockSpec(memory_space=pltpu.SMEM)
    hbm = pl.BlockSpec(memory_space=pltpu.HBM)
    return pl.pallas_call(
        functools.partial(kernel, depth_count, probe_count),
        out_shape=jax.ShapeDtypeStruct((2, 1, rows, columns), F32),
        in_specs=[hbm, hbm, hbm, smem, smem, hbm],
        out_specs=vmem,
        scratch_shapes=[
            pltpu.VMEM(waves.shape, waves.dtype),
            pltpu.VMEM(layers.shape, layers.dtype),
            pltpu.VMEM(residual.shape, residual.dtype),
            pltpu.VMEM(table.shape, BF16),
            pltpu.VMEM((2, side, side), BF16),
            pltpu.VMEM((2, side, side), BF16),
            pltpu.VMEM((2, side, 2 * side), BF16),
            pltpu.VMEM((2, 2, side, side), BF16),
            pltpu.VMEM((2, 16, side), jnp.int32),
            pltpu.VMEM((probe_count - 1, 2, rows, columns), BF16),
            pltpu.VMEM((probe_count - 1, 2, rows, columns), BF16),
            pltpu.SemaphoreType.DMA((4,)),
            pltpu.SemaphoreType.DMA((2, CHUNKS)),
            pltpu.SemaphoreType.DMA((2, CHUNKS)),
            pltpu.SemaphoreType.DMA((2,)),
            pltpu.SemaphoreType.DMA((2, probe_count - 1)),
        ],
        compiler_params=pltpu.CompilerParams(
            collective_id=0, has_side_effects=True, vmem_limit_bytes=60 * 1024 * 1024
        ),
    )(waves, layers, residual, offsets, slot, jnp.asarray(table))


def solution(mesh):
    return jax.shard_map(
        functools.partial(per_device, mesh.shape["depth"], mesh.shape["probe"], mesh.shape["tile"]),
        mesh=mesh,
        in_specs=(
            P("depth", ("groups", "probe", "tile"), None, None, None),
            P("depth", ("groups", "probe", "tile"), None, None, None),
            P(("groups", "probe", "tile"), None, None, None),
            P("groups", None),
            P(("groups", "probe", "tile")),
        ),
        out_specs=P("groups", "depth", "probe", "tile"),
        check_vma=False,
    )
```

```python
import functools

import jax
import jax.numpy as jnp
import ml_dtypes
import numpy as np
from jax import lax
from jax.experimental import pallas as pl
from jax.experimental.pallas import tpu as pltpu
from jax.sharding import PartitionSpec as P

OBJ = 512
CHUNKS = 4
MESH = pl.DeviceIdType.MESH
F32 = jnp.float32
BF16 = jnp.bfloat16


def propagator(side):
    counter = np.arange(side)
    frequency = (counter + side // 2) % side - side // 2
    chirp = np.exp(0.5j * frequency.astype(np.float64) ** 2 / side)
    column = np.fft.ifft(chirp)
    matrix = column[(counter[:, None] - counter[None, :]) % side]
    parts = np.concatenate([matrix.real, matrix.imag], axis=1)
    high = parts.astype(ml_dtypes.bfloat16)
    low = (parts - high.astype(np.float64)).astype(ml_dtypes.bfloat16)
    return np.stack([high, low])


def dot(a, b):
    return jnp.dot(a, b, preferred_element_type=F32)


def split(value):
    high = value.astype(BF16)
    return high, (value - high.astype(F32)).astype(BF16)


def conj_times(layer_real, layer_imag, real, imag):
    return (
        layer_real * real + layer_imag * imag,
        layer_real * imag - layer_imag * real,
    )


def flip(index, mask, count):
    result, bit = 0, 1
    while bit < count:
        result = result + ((index // bit + (mask // bit) % 2) % 2) * bit
        bit *= 2
    return result


def kernel(
    depth_count,
    probe_count,
    waves_hbm,
    layers_hbm,
    residual_hbm,
    offsets,
    slot,
    table_hbm,
    out,
    waves,
    layers,
    residual,
    table,
    hand_out,
    hand_in,
    turned,
    grads,
    corners,
    pair_out,
    pair_in,
    strips_out,
    strips_in,
    load_sems,
    hand_sems,
    grad_sems,
    corner_sems,
    pair_sems,
    strip_sems,
):
    side = waves.shape[-1]
    rows, columns = out.shape[2], out.shape[3]
    step = side // CHUNKS
    depth = lax.axis_index("depth")
    probe = lax.axis_index("probe")
    tile = lax.axis_index("tile")
    partner = flip(probe, 1, probe_count)
    is_top = depth == depth_count - 1
    has_below = depth > 0

    barrier = pltpu.get_barrier_semaphore()
    for mask in [1, *range(2, probe_count, 2)]:
        pl.semaphore_signal(
            barrier, inc=1, device_id={"probe": flip(probe, mask, probe_count)}, device_id_type=MESH
        )
    pl.semaphore_signal(barrier, inc=1, device_id={"tile": 1 - tile}, device_id_type=MESH)

    @pl.when(depth < depth_count - 1)
    def _():
        pl.semaphore_signal(barrier, inc=1, device_id={"depth": depth + 1}, device_id_type=MESH)

    load_residual = pltpu.make_async_copy(residual_hbm, residual, load_sems.at[0])
    load_layers = pltpu.make_async_copy(layers_hbm, layers, load_sems.at[1])
    load_waves = pltpu.make_async_copy(waves_hbm, waves, load_sems.at[2])
    load_table = pltpu.make_async_copy(table_hbm, table, load_sems.at[3])

    @pl.when(is_top)
    def _():
        load_residual.start()

    if depth_count > 1:

        @pl.when(has_below)
        def _():
            load_layers.start()

        @pl.when(jnp.logical_not(is_top))
        def _():
            load_table.start()

    load_waves.start()

    own_slot = slot[0]
    top_row = offsets[0, own_slot]
    left_column = offsets[1, own_slot]
    corners[0, 0:8, :] = jnp.full((8, side), top_row, jnp.int32)
    corners[0, 8:16, :] = jnp.full((8, side), left_column, jnp.int32)

    @pl.when(has_below)
    def _():
        pl.semaphore_wait(barrier, probe_count // 2 + 2)

    @pl.when(jnp.logical_not(has_below))
    def _():
        pl.semaphore_wait(barrier, probe_count // 2 + 1)

    corner_copy = pltpu.make_async_remote_copy(
        src_ref=corners.at[0],
        dst_ref=corners.at[1],
        send_sem=corner_sems.at[0],
        recv_sem=corner_sems.at[1],
        device_id={"tile": 1 - tile},
        device_id_type=MESH,
    )
    corner_copy.start()

    def hand_copy(part):
        window = pl.ds(part * step, step)
        return pltpu.make_async_remote_copy(
            src_ref=hand_out.at[:, window, :],
            dst_ref=hand_in.at[:, window, :],
            send_sem=hand_sems.at[0, part],
            recv_sem=hand_sems.at[1, part],
            device_id={"depth": depth - 1},
            device_id_type=MESH,
        )

    def grad_copy(part):
        window = pl.ds(part * step, step)
        return pltpu.make_async_remote_copy(
            src_ref=grads.at[0, :, window, :],
            dst_ref=grads.at[1, :, window, :],
            send_sem=grad_sems.at[0, part],
            recv_sem=grad_sems.at[1, part],
            device_id={"tile": 1 - tile},
            device_id_type=MESH,
        )

    def hand_down(part, real, imag):
        window = pl.ds(part * step, step)
        handed = conj_times(
            layers[0, 0, 0, window, :].astype(F32), layers[0, 0, 1, window, :].astype(F32), real, imag
        )
        hand_out[0, window, :] = handed[0].astype(BF16)
        hand_out[1, window, :] = handed[1].astype(BF16)
        hand_copy(part).start()

    def give_gradient(part, real, imag):
        window = pl.ds(part * step, step)
        gradient = conj_times(
            waves[0, 0, 0, window, :].astype(F32), waves[0, 0, 1, window, :].astype(F32), real, imag
        )
        grads[0, 0, window, :] = gradient[0].astype(BF16)
        grads[0, 1, window, :] = gradient[1].astype(BF16)
        grad_copy(part).start()

    @pl.when(is_top)
    def _():
        load_residual.wait()
        if depth_count > 1:
            load_layers.wait()
            for part in range(CHUNKS):
                window = pl.ds(part * step, step)
                hand_down(part, residual[0, 0, window, :], residual[0, 1, window, :])
        load_waves.wait()
        for part in range(CHUNKS):
            window = pl.ds(part * step, step)
            give_gradient(part, residual[0, 0, window, :], residual[0, 1, window, :])

    if depth_count > 1:

        @pl.when(jnp.logical_not(is_top))
        def _():
            load_table.wait()
            load_waves.wait()
            if depth_count > 2:

                @pl.when(has_below)
                def _():
                    load_layers.wait()

            for part in range(CHUNKS):
                window = pl.ds(part * step, step)
                hand_copy(part).wait_recv()
                real = dot(hand_in[0, window, :], table[0]) + dot(hand_in[0, window, :], table[1])
                imag = dot(hand_in[1, window, :], table[0]) + dot(hand_in[1, window, :], table[1])
                product = real[:, :side] - imag[:, side:], real[:, side:] + imag[:, :side]
                for c in range(2):
                    top, rest = split(product[c])
                    turned[0, window, pl.ds(c * side, side)] = top
                    turned[1, window, pl.ds(c * side, side)] = rest

            for part in range(CHUNKS):
                window = pl.ds(part * step, step)

                def from_left(index):
                    columns = pl.ds(index * side, side)
                    return (
                        dot(table[0, window, columns], turned[0])
                        + dot(table[1, window, columns], turned[0])
                        + dot(table[0, window, columns], turned[1])
                    )

                by_real, by_imag = from_left(0), from_left(1)
                real = by_real[:, :side] - by_imag[:, side:]
                imag = by_real[:, side:] + by_imag[:, :side]
                if depth_count > 2:

                    @pl.when(has_below)
                    def _():
                        hand_down(part, real, imag)

                give_gradient(part, real, imag)

    row_index = lax.broadcasted_iota(jnp.int32, (side, columns), 0)
    column_index = lax.broadcasted_iota(jnp.int32, (side, columns), 1) + tile * columns

    def onehot(match):
        return jnp.where(match, 1.0, 0.0).astype(BF16)

    own_columns = onehot(column_index - row_index == left_column)
    placed = [[dot(grads[0, c], own_columns).astype(BF16)] for c in range(2)]

    corner_copy.wait_recv()
    for part in range(CHUNKS):
        grad_copy(part).wait_recv()
    peer_row = corners[1, 0:1, :]
    peer_columns = onehot(column_index - row_index == corners[1, 8:9, 0:columns])
    for c in range(2):
        placed[c].append(dot(grads[1, c], peer_columns).astype(BF16))

    strip_row = lax.broadcasted_iota(jnp.int32, (rows, side), 0)
    patch_row = lax.broadcasted_iota(jnp.int32, (rows, side), 1)
    distance = strip_row - patch_row

    def strip(owner):
        shifted = distance + owner * rows
        own_rows = onehot(shifted == top_row)
        peer_rows = onehot(shifted == peer_row)
        return [dot(own_rows, placed[c][0]) + dot(peer_rows, placed[c][1]) for c in range(2)]

    def pair_copy(mask, c):
        return pltpu.make_async_remote_copy(
            src_ref=pair_out.at[mask // 2, c],
            dst_ref=pair_in.at[mask // 2, c],
            send_sem=pair_sems.at[0, mask // 2, c],
            recv_sem=pair_sems.at[1, mask // 2, c],
            device_id={"probe": partner},
            device_id_type=MESH,
        )

    def strip_copy(mask, c):
        return pltpu.make_async_remote_copy(
            src_ref=strips_out.at[mask // 2 - 1, c],
            dst_ref=strips_in.at[mask // 2 - 1, c],
            send_sem=strip_sems.at[0, mask // 2 - 1, c],
            recv_sem=strip_sems.at[1, mask // 2 - 1, c],
            device_id={"probe": flip(probe, mask, probe_count)},
            device_id_type=MESH,
        )

    for mask in range(probe_count - 2, -1, -2):
        value = strip(flip(partner, mask, probe_count))
        for c in range(2):
            pair_out[mask // 2, c] = value[c].astype(BF16)
            pair_copy(mask, c).start()
    for mask in range(probe_count - 2, 0, -2):
        value = strip(flip(probe, mask, probe_count))
        for c in range(2):
            pair_copy(mask, c).wait_recv()
            strips_out[mask // 2 - 1, c] = (value[c] + pair_in[mask // 2, c].astype(F32)).astype(BF16)
            strip_copy(mask, c).start()
    total = strip(probe)
    for c in range(2):
        pair_copy(0, c).wait_recv()
        out[c, 0] = total[c] + pair_in[0, c].astype(F32)
    for mask in range(probe_count - 2, 0, -2):
        for c in range(2):
            strip_copy(mask, c).wait_recv()
            out[c, 0] += strips_in[mask // 2 - 1, c].astype(F32)

    corner_copy.wait_send()
    for part in range(CHUNKS):
        grad_copy(part).wait_send()
    for mask in range(0, probe_count, 2):
        for c in range(2):
            pair_copy(mask, c).wait_send()
    for mask in range(2, probe_count, 2):
        for c in range(2):
            strip_copy(mask, c).wait_send()

    @pl.when(has_below)
    def _():
        for part in range(CHUNKS):
            hand_copy(part).wait_send()


def per_device(depth_count, probe_count, tile_count, waves, layers, residual, offsets, slot):
    side = waves.shape[-1]
    table = propagator(side)
    rows, columns = OBJ // probe_count, OBJ // tile_count
    vmem = pl.BlockSpec(memory_space=pltpu.VMEM)
    smem = pl.BlockSpec(memory_space=pltpu.SMEM)
    hbm = pl.BlockSpec(memory_space=pltpu.HBM)
    return pl.pallas_call(
        functools.partial(kernel, depth_count, probe_count),
        out_shape=jax.ShapeDtypeStruct((2, 1, rows, columns), F32),
        in_specs=[hbm, hbm, hbm, smem, smem, hbm],
        out_specs=vmem,
        scratch_shapes=[
            pltpu.VMEM(waves.shape, waves.dtype),
            pltpu.VMEM(layers.shape, layers.dtype),
            pltpu.VMEM(residual.shape, residual.dtype),
            pltpu.VMEM(table.shape, BF16),
            pltpu.VMEM((2, side, side), BF16),
            pltpu.VMEM((2, side, side), BF16),
            pltpu.VMEM((2, side, 2 * side), BF16),
            pltpu.VMEM((2, 2, side, side), BF16),
            pltpu.VMEM((2, 16, side), jnp.int32),
            pltpu.VMEM((probe_count // 2, 2, rows, columns), BF16),
            pltpu.VMEM((probe_count // 2, 2, rows, columns), BF16),
            pltpu.VMEM((probe_count // 2 - 1, 2, rows, columns), BF16),
            pltpu.VMEM((probe_count // 2 - 1, 2, rows, columns), BF16),
            pltpu.SemaphoreType.DMA((4,)),
            pltpu.SemaphoreType.DMA((2, CHUNKS)),
            pltpu.SemaphoreType.DMA((2, CHUNKS)),
            pltpu.SemaphoreType.DMA((2,)),
            pltpu.SemaphoreType.DMA((2, probe_count // 2, 2)),
            pltpu.SemaphoreType.DMA((2, probe_count // 2 - 1, 2)),
        ],
        compiler_params=pltpu.CompilerParams(
            collective_id=0, has_side_effects=True, vmem_limit_bytes=60 * 1024 * 1024
        ),
    )(waves, layers, residual, offsets.T, slot, jnp.asarray(table))


def solution(mesh):
    return jax.shard_map(
        functools.partial(per_device, mesh.shape["depth"], mesh.shape["probe"], mesh.shape["tile"]),
        mesh=mesh,
        in_specs=(
            P("depth", ("groups", "probe", "tile"), None, None, None),
            P("depth", ("groups", "probe", "tile"), None, None, None),
            P(("groups", "probe", "tile"), None, None, None),
            P("groups", None),
            P(("groups", "probe", "tile")),
        ),
        out_specs=P("groups", "depth", "probe", "tile"),
        check_vma=False,
    )
```

```python
import functools

import jax
import jax.numpy as jnp
import ml_dtypes
import numpy as np
from jax import lax
from jax.experimental import pallas as pl
from jax.experimental.pallas import tpu as pltpu
from jax.sharding import PartitionSpec as P

OBJ = 512
CHUNKS = 2
MESH = pl.DeviceIdType.MESH
F32 = jnp.float32
BF16 = jnp.bfloat16


def propagator(side):
    counter = np.arange(side)
    frequency = (counter + side // 2) % side - side // 2
    chirp = np.exp(0.5j * frequency.astype(np.float64) ** 2 / side)
    column = np.fft.ifft(chirp)
    matrix = column[(counter[:, None] - counter[None, :]) % side]
    parts = np.concatenate([matrix.real, matrix.imag], axis=1)
    high = parts.astype(ml_dtypes.bfloat16)
    low = (parts - high.astype(np.float64)).astype(ml_dtypes.bfloat16)
    return np.stack([high, low])


def dot(a, b):
    return jnp.dot(a, b, preferred_element_type=F32)


def split(value):
    high = value.astype(BF16)
    return high, (value - high.astype(F32)).astype(BF16)


def conj_times(layer_real, layer_imag, real, imag):
    return (
        layer_real * real + layer_imag * imag,
        layer_real * imag - layer_imag * real,
    )


def flip(index, mask, count):
    result, bit = 0, 1
    while bit < count:
        result = result + ((index // bit + (mask // bit) % 2) % 2) * bit
        bit *= 2
    return result


def kernel(
    depth_count,
    probe_count,
    waves_hbm,
    layers_hbm,
    residual_hbm,
    offsets,
    slot,
    table_hbm,
    out,
    waves,
    layers,
    residual,
    table,
    hand_out,
    hand_in,
    turned,
    grads,
    corners,
    direct_out,
    direct_in,
    pair_out,
    pair_in,
    sum_out,
    sum_in,
    held,
    load_sems,
    hand_sems,
    grad_sems,
    corner_sems,
    direct_sems,
    pair_sems,
    sum_sems,
):
    side = waves.shape[-1]
    rows, columns = out.shape[2], out.shape[3]
    step = side // CHUNKS
    depth = lax.axis_index("depth")
    probe = lax.axis_index("probe")
    tile = lax.axis_index("tile")
    is_top = depth == depth_count - 1
    has_below = depth > 0

    barrier = pltpu.get_barrier_semaphore()
    for mask in range(1, probe_count):
        pl.semaphore_signal(
            barrier, inc=1, device_id={"probe": flip(probe, mask, probe_count)}, device_id_type=MESH
        )
    pl.semaphore_signal(barrier, inc=1, device_id={"tile": 1 - tile}, device_id_type=MESH)

    @pl.when(depth < depth_count - 1)
    def _():
        pl.semaphore_signal(barrier, inc=1, device_id={"depth": depth + 1}, device_id_type=MESH)

    load_residual = pltpu.make_async_copy(residual_hbm, residual, load_sems.at[0])
    load_layers = pltpu.make_async_copy(layers_hbm, layers, load_sems.at[1])
    load_waves = pltpu.make_async_copy(waves_hbm, waves, load_sems.at[2])
    load_table = pltpu.make_async_copy(table_hbm, table, load_sems.at[3])

    @pl.when(is_top)
    def _():
        load_residual.start()

    if depth_count > 1:

        @pl.when(has_below)
        def _():
            load_layers.start()

        @pl.when(jnp.logical_not(is_top))
        def _():
            load_table.start()

    load_waves.start()

    own_slot = slot[0]
    top_row = offsets[0, own_slot]
    left_column = offsets[1, own_slot]
    corners[0, 0:8, :] = jnp.full((8, side), top_row, jnp.int32)
    corners[0, 8:16, :] = jnp.full((8, side), left_column, jnp.int32)

    @pl.when(has_below)
    def _():
        pl.semaphore_wait(barrier, probe_count + 1)

    @pl.when(jnp.logical_not(has_below))
    def _():
        pl.semaphore_wait(barrier, probe_count)

    corner_copy = pltpu.make_async_remote_copy(
        src_ref=corners.at[0],
        dst_ref=corners.at[1],
        send_sem=corner_sems.at[0],
        recv_sem=corner_sems.at[1],
        device_id={"tile": 1 - tile},
        device_id_type=MESH,
    )
    corner_copy.start()

    def hand_copy(part):
        window = pl.ds(part * step, step)
        return pltpu.make_async_remote_copy(
            src_ref=hand_out.at[:, window, :],
            dst_ref=hand_in.at[:, window, :],
            send_sem=hand_sems.at[0, part],
            recv_sem=hand_sems.at[1, part],
            device_id={"depth": depth - 1},
            device_id_type=MESH,
        )

    def grad_copy(part):
        window = pl.ds(part * step, step)
        return pltpu.make_async_remote_copy(
            src_ref=grads.at[0, :, window, :],
            dst_ref=grads.at[1, :, window, :],
            send_sem=grad_sems.at[0, part],
            recv_sem=grad_sems.at[1, part],
            device_id={"tile": 1 - tile},
            device_id_type=MESH,
        )

    def hand_down(part, real, imag):
        window = pl.ds(part * step, step)
        handed = conj_times(
            layers[0, 0, 0, window, :].astype(F32), layers[0, 0, 1, window, :].astype(F32), real, imag
        )
        hand_out[0, window, :] = handed[0].astype(BF16)
        hand_out[1, window, :] = handed[1].astype(BF16)
        hand_copy(part).start()

    def give_gradient(part, real, imag):
        window = pl.ds(part * step, step)
        gradient = conj_times(
            waves[0, 0, 0, window, :].astype(F32), waves[0, 0, 1, window, :].astype(F32), real, imag
        )
        grads[0, 0, window, :] = gradient[0].astype(BF16)
        grads[0, 1, window, :] = gradient[1].astype(BF16)
        grad_copy(part).start()

    @pl.when(is_top)
    def _():
        load_residual.wait()
        if depth_count > 1:
            load_layers.wait()
            for part in range(CHUNKS):
                window = pl.ds(part * step, step)
                hand_down(part, residual[0, 0, window, :], residual[0, 1, window, :])
        load_waves.wait()
        for part in range(CHUNKS):
            window = pl.ds(part * step, step)
            give_gradient(part, residual[0, 0, window, :], residual[0, 1, window, :])

    if depth_count > 1:

        @pl.when(jnp.logical_not(is_top))
        def _():
            load_table.wait()
            load_waves.wait()
            if depth_count > 2:

                @pl.when(has_below)
                def _():
                    load_layers.wait()

            for part in range(CHUNKS):
                window = pl.ds(part * step, step)
                hand_copy(part).wait_recv()
                real = dot(hand_in[0, window, :], table[0]) + dot(hand_in[0, window, :], table[1])
                imag = dot(hand_in[1, window, :], table[0]) + dot(hand_in[1, window, :], table[1])
                product = real[:, :side] - imag[:, side:], real[:, side:] + imag[:, :side]
                for c in range(2):
                    top, rest = split(product[c])
                    turned[0, window, pl.ds(c * side, side)] = top
                    turned[1, window, pl.ds(c * side, side)] = rest

            for part in range(CHUNKS):
                window = pl.ds(part * step, step)

                def from_left(index):
                    columns = pl.ds(index * side, side)
                    return (
                        dot(table[0, window, columns], turned[0])
                        + dot(table[1, window, columns], turned[0])
                        + dot(table[0, window, columns], turned[1])
                    )

                by_real, by_imag = from_left(0), from_left(1)
                real = by_real[:, :side] - by_imag[:, side:]
                imag = by_real[:, side:] + by_imag[:, :side]
                if depth_count > 2:

                    @pl.when(has_below)
                    def _():
                        hand_down(part, real, imag)

                give_gradient(part, real, imag)

    row_index = lax.broadcasted_iota(jnp.int32, (side, columns), 0)
    column_index = lax.broadcasted_iota(jnp.int32, (side, columns), 1) + tile * columns

    def onehot(match):
        return jnp.where(match, 1.0, 0.0).astype(BF16)

    own_columns = onehot(column_index - row_index == left_column)
    placed = [[dot(grads[0, c], own_columns).astype(BF16)] for c in range(2)]

    corner_copy.wait_recv()
    for part in range(CHUNKS):
        grad_copy(part).wait_recv()
    peer_row = corners[1, 0:1, :]
    peer_columns = onehot(column_index - row_index == corners[1, 8:9, 0:columns])
    for c in range(2):
        placed[c].append(dot(grads[1, c], peer_columns).astype(BF16))

    strip_row = lax.broadcasted_iota(jnp.int32, (rows, side), 0)
    patch_row = lax.broadcasted_iota(jnp.int32, (rows, side), 1)
    distance = strip_row - patch_row

    def strip(owner):
        shifted = distance + owner * rows
        own_rows = onehot(shifted == top_row)
        peer_rows = onehot(shifted == peer_row)
        return [dot(own_rows, placed[c][0]) + dot(peer_rows, placed[c][1]) for c in range(2)]

    def direct_copy(mask, c):
        place = mask - 1 if c == 0 else probe_count - 1
        return pltpu.make_async_remote_copy(
            src_ref=direct_out.at[place],
            dst_ref=direct_in.at[place],
            send_sem=direct_sems.at[0, place],
            recv_sem=direct_sems.at[1, place],
            device_id={"probe": flip(probe, mask, probe_count)},
            device_id_type=MESH,
        )

    def pair_copy(place):
        return pltpu.make_async_remote_copy(
            src_ref=pair_out.at[place],
            dst_ref=pair_in.at[place],
            send_sem=pair_sems.at[0, place],
            recv_sem=pair_sems.at[1, place],
            device_id={"probe": flip(probe, 1, probe_count)},
            device_id_type=MESH,
        )

    def sum_copy(place):
        return pltpu.make_async_remote_copy(
            src_ref=sum_out.at[place],
            dst_ref=sum_in.at[place],
            send_sem=sum_sems.at[0, place],
            recv_sem=sum_sems.at[1, place],
            device_id={"probe": flip(probe, 2 * place + 2, probe_count)},
            device_id_type=MESH,
        )

    others = range(probe_count // 2 - 1, 0, -1)
    for other in others:
        mask = 2 * other + 1
        real, imag = strip(flip(probe, mask, probe_count))
        pair_out[other - 1] = imag.astype(BF16)
        pair_copy(other - 1).start()
        direct_out[mask - 1] = real.astype(BF16)
        direct_copy(mask, 0).start()
    for other in others:
        mask = 2 * other
        real, imag = strip(flip(probe, mask, probe_count))
        direct_out[mask - 1] = real.astype(BF16)
        direct_copy(mask, 0).start()
        held[other - 1] = imag
    real, imag = strip(flip(probe, 1, probe_count))
    direct_out[0] = real.astype(BF16)
    direct_out[probe_count - 1] = imag.astype(BF16)
    for other in others:
        pair_copy(other - 1).wait_recv()
        sum_out[other - 1] = (held[other - 1] + pair_in[other - 1].astype(F32)).astype(BF16)
        sum_copy(other - 1).start()
    direct_copy(1, 0).start()
    direct_copy(1, 1).start()
    total = strip(probe)
    for c in range(2):
        out[c, 0] = total[c]
    for mask in range(probe_count - 1, 0, -1):
        direct_copy(mask, 0).wait_recv()
        out[0, 0] += direct_in[mask - 1].astype(F32)
    direct_copy(1, 1).wait_recv()
    out[1, 0] += direct_in[probe_count - 1].astype(F32)
    for other in others:
        sum_copy(other - 1).wait_recv()
        out[1, 0] += sum_in[other - 1].astype(F32)

    corner_copy.wait_send()
    for part in range(CHUNKS):
        grad_copy(part).wait_send()
    for mask in range(1, probe_count):
        direct_copy(mask, 0).wait_send()
    direct_copy(1, 1).wait_send()
    for other in others:
        pair_copy(other - 1).wait_send()
        sum_copy(other - 1).wait_send()

    @pl.when(has_below)
    def _():
        for part in range(CHUNKS):
            hand_copy(part).wait_send()


def per_device(depth_count, probe_count, tile_count, waves, layers, residual, offsets, slot):
    side = waves.shape[-1]
    table = propagator(side)
    rows, columns = OBJ // probe_count, OBJ // tile_count
    others = probe_count // 2 - 1
    vmem = pl.BlockSpec(memory_space=pltpu.VMEM)
    smem = pl.BlockSpec(memory_space=pltpu.SMEM)
    hbm = pl.BlockSpec(memory_space=pltpu.HBM)
    return pl.pallas_call(
        functools.partial(kernel, depth_count, probe_count),
        out_shape=jax.ShapeDtypeStruct((2, 1, rows, columns), F32),
        in_specs=[hbm, hbm, hbm, smem, smem, hbm],
        out_specs=vmem,
        scratch_shapes=[
            pltpu.VMEM(waves.shape, waves.dtype),
            pltpu.VMEM(layers.shape, layers.dtype),
            pltpu.VMEM(residual.shape, residual.dtype),
            pltpu.VMEM(table.shape, BF16),
            pltpu.VMEM((2, side, side), BF16),
            pltpu.VMEM((2, side, side), BF16),
            pltpu.VMEM((2, side, 2 * side), BF16),
            pltpu.VMEM((2, 2, side, side), BF16),
            pltpu.VMEM((2, 16, side), jnp.int32),
            pltpu.VMEM((probe_count, rows, columns), BF16),
            pltpu.VMEM((probe_count, rows, columns), BF16),
            pltpu.VMEM((others, rows, columns), BF16),
            pltpu.VMEM((others, rows, columns), BF16),
            pltpu.VMEM((others, rows, columns), BF16),
            pltpu.VMEM((others, rows, columns), BF16),
            pltpu.VMEM((others, rows, columns), F32),
            pltpu.SemaphoreType.DMA((4,)),
            pltpu.SemaphoreType.DMA((2, CHUNKS)),
            pltpu.SemaphoreType.DMA((2, CHUNKS)),
            pltpu.SemaphoreType.DMA((2,)),
            pltpu.SemaphoreType.DMA((2, probe_count)),
            pltpu.SemaphoreType.DMA((2, others)),
            pltpu.SemaphoreType.DMA((2, others)),
        ],
        compiler_params=pltpu.CompilerParams(
            collective_id=0, has_side_effects=True, vmem_limit_bytes=32 * 1024 * 1024
        ),
    )(
        *(pltpu.with_memory_space_constraint(x, pltpu.HBM) for x in (waves, layers, residual)),
        offsets.T,
        slot,
        pltpu.with_memory_space_constraint(jnp.asarray(table), pltpu.HBM),
    )


def solution(mesh):
    return jax.shard_map(
        functools.partial(per_device, mesh.shape["depth"], mesh.shape["probe"], mesh.shape["tile"]),
        mesh=mesh,
        in_specs=(
            P("depth", ("groups", "probe", "tile"), None, None, None),
            P("depth", ("groups", "probe", "tile"), None, None, None),
            P(("groups", "probe", "tile"), None, None, None),
            P("groups", None),
            P(("groups", "probe", "tile")),
        ),
        out_specs=P("groups", "depth", "probe", "tile"),
        check_vma=False,
    )
```

```python
import functools

import jax
import jax.numpy as jnp
import ml_dtypes
import numpy as np
from jax import lax
from jax.experimental import pallas as pl
from jax.experimental.pallas import tpu as pltpu
from jax.sharding import PartitionSpec as P

OBJ = 512
CHUNKS = 1
MESH = pl.DeviceIdType.MESH
F32 = jnp.float32
BF16 = jnp.bfloat16


def propagator(side):
    counter = np.arange(side)
    frequency = (counter + side // 2) % side - side // 2
    chirp = np.exp(0.5j * frequency.astype(np.float64) ** 2 / side)
    column = np.fft.ifft(chirp)
    matrix = column[(counter[:, None] - counter[None, :]) % side]
    parts = np.concatenate([matrix.real, matrix.imag], axis=1)
    high = parts.astype(ml_dtypes.bfloat16)
    low = (parts - high.astype(np.float64)).astype(ml_dtypes.bfloat16)
    return np.stack([high, low])


def dot(a, b):
    return jnp.dot(a, b, preferred_element_type=F32)


def split(value):
    high = value.astype(BF16)
    return high, (value - high.astype(F32)).astype(BF16)


def conj_times(layer_real, layer_imag, real, imag):
    return (
        layer_real * real + layer_imag * imag,
        layer_real * imag - layer_imag * real,
    )


def flip(index, mask, count):
    result, bit = 0, 1
    while bit < count:
        result = result + ((index // bit + (mask // bit) % 2) % 2) * bit
        bit *= 2
    return result


def kernel(
    depth_count,
    probe_count,
    waves_hbm,
    layers_hbm,
    residual_hbm,
    offsets,
    slot,
    table_hbm,
    out,
    waves,
    layers,
    residual,
    table,
    hand_out,
    hand_in,
    turned,
    grads,
    corners,
    direct_out,
    direct_in,
    pair_out,
    pair_in,
    sum_out,
    sum_in,
    held,
    load_sems,
    hand_sems,
    grad_sems,
    corner_sems,
    direct_sems,
    pair_sems,
    sum_sems,
):
    side = waves.shape[-1]
    rows, columns = out.shape[2], out.shape[3]
    step = side // CHUNKS
    depth = lax.axis_index("depth")
    probe = lax.axis_index("probe")
    tile = lax.axis_index("tile")
    is_top = depth == depth_count - 1
    has_below = depth > 0

    barrier = pltpu.get_barrier_semaphore()
    for mask in range(1, probe_count):
        pl.semaphore_signal(
            barrier, inc=1, device_id={"probe": flip(probe, mask, probe_count)}, device_id_type=MESH
        )
    pl.semaphore_signal(barrier, inc=1, device_id={"tile": 1 - tile}, device_id_type=MESH)

    @pl.when(depth < depth_count - 1)
    def _():
        pl.semaphore_signal(barrier, inc=1, device_id={"depth": depth + 1}, device_id_type=MESH)

    load_residual = pltpu.make_async_copy(residual_hbm, residual, load_sems.at[0])
    load_layers = pltpu.make_async_copy(layers_hbm, layers, load_sems.at[1])
    load_waves = pltpu.make_async_copy(waves_hbm, waves, load_sems.at[2])
    load_table = pltpu.make_async_copy(table_hbm, table, load_sems.at[3])

    @pl.when(is_top)
    def _():
        load_residual.start()

    if depth_count > 1:

        @pl.when(has_below)
        def _():
            load_layers.start()

        @pl.when(jnp.logical_not(is_top))
        def _():
            load_table.start()

    load_waves.start()

    own_slot = slot[0]
    top_row = offsets[0, own_slot]
    left_column = offsets[1, own_slot]
    corners[0, 0:8, :] = jnp.full((8, side), top_row, jnp.int32)
    corners[0, 8:16, :] = jnp.full((8, side), left_column, jnp.int32)

    @pl.when(has_below)
    def _():
        pl.semaphore_wait(barrier, probe_count + 1)

    @pl.when(jnp.logical_not(has_below))
    def _():
        pl.semaphore_wait(barrier, probe_count)

    corner_copy = pltpu.make_async_remote_copy(
        src_ref=corners.at[0],
        dst_ref=corners.at[1],
        send_sem=corner_sems.at[0],
        recv_sem=corner_sems.at[1],
        device_id={"tile": 1 - tile},
        device_id_type=MESH,
    )
    corner_copy.start()

    def hand_copy(part):
        window = pl.ds(part * step, step)
        return pltpu.make_async_remote_copy(
            src_ref=hand_out.at[:, window, :],
            dst_ref=hand_in.at[:, window, :],
            send_sem=hand_sems.at[0, part],
            recv_sem=hand_sems.at[1, part],
            device_id={"depth": depth - 1},
            device_id_type=MESH,
        )

    def grad_copy(part):
        window = pl.ds(part * step, step)
        return pltpu.make_async_remote_copy(
            src_ref=grads.at[0, :, window, :],
            dst_ref=grads.at[1, :, window, :],
            send_sem=grad_sems.at[0, part],
            recv_sem=grad_sems.at[1, part],
            device_id={"tile": 1 - tile},
            device_id_type=MESH,
        )

    def hand_down(part, real, imag):
        window = pl.ds(part * step, step)
        handed = conj_times(
            layers[0, 0, 0, window, :].astype(F32), layers[0, 0, 1, window, :].astype(F32), real, imag
        )
        hand_out[0, window, :] = handed[0].astype(BF16)
        hand_out[1, window, :] = handed[1].astype(BF16)
        hand_copy(part).start()

    def give_gradient(part, real, imag):
        window = pl.ds(part * step, step)
        gradient = conj_times(
            waves[0, 0, 0, window, :].astype(F32), waves[0, 0, 1, window, :].astype(F32), real, imag
        )
        grads[0, 0, window, :] = gradient[0].astype(BF16)
        grads[0, 1, window, :] = gradient[1].astype(BF16)
        grad_copy(part).start()

    @pl.when(is_top)
    def _():
        load_residual.wait()
        if depth_count > 1:
            load_layers.wait()
            for part in range(CHUNKS):
                window = pl.ds(part * step, step)
                hand_down(part, residual[0, 0, window, :], residual[0, 1, window, :])
        load_waves.wait()
        for part in range(CHUNKS):
            window = pl.ds(part * step, step)
            give_gradient(part, residual[0, 0, window, :], residual[0, 1, window, :])

    if depth_count > 1:

        @pl.when(jnp.logical_not(is_top))
        def _():
            load_table.wait()
            load_waves.wait()
            if depth_count > 2:

                @pl.when(has_below)
                def _():
                    load_layers.wait()

            for part in range(CHUNKS):
                window = pl.ds(part * step, step)
                hand_copy(part).wait_recv()
                real = dot(hand_in[0, window, :], table[0]) + dot(hand_in[0, window, :], table[1])
                imag = dot(hand_in[1, window, :], table[0]) + dot(hand_in[1, window, :], table[1])
                product = real[:, :side] - imag[:, side:], real[:, side:] + imag[:, :side]
                for c in range(2):
                    turned[window, pl.ds(c * side, side)] = product[c].astype(BF16)

            for part in range(CHUNKS):
                window = pl.ds(part * step, step)

                def from_left(index):
                    columns = pl.ds(index * side, side)
                    return (
                        dot(table[0, window, columns], turned[...]) + dot(table[1, window, columns], turned[...])
                    )

                by_real, by_imag = from_left(0), from_left(1)
                real = by_real[:, :side] - by_imag[:, side:]
                imag = by_real[:, side:] + by_imag[:, :side]
                if depth_count > 2:

                    @pl.when(has_below)
                    def _():
                        hand_down(part, real, imag)

                give_gradient(part, real, imag)

    row_index = lax.broadcasted_iota(jnp.int32, (side, columns), 0)
    column_index = lax.broadcasted_iota(jnp.int32, (side, columns), 1) + tile * columns

    def onehot(match):
        return jnp.where(match, 1.0, 0.0).astype(BF16)

    own_columns = onehot(column_index - row_index == left_column)
    placed = [[dot(grads[0, c], own_columns).astype(BF16)] for c in range(2)]

    corner_copy.wait_recv()
    for part in range(CHUNKS):
        grad_copy(part).wait_recv()
    peer_row = corners[1, 0:1, :]
    peer_columns = onehot(column_index - row_index == corners[1, 8:9, 0:columns])
    for c in range(2):
        placed[c].append(dot(grads[1, c], peer_columns).astype(BF16))

    strip_row = lax.broadcasted_iota(jnp.int32, (rows, side), 0)
    patch_row = lax.broadcasted_iota(jnp.int32, (rows, side), 1)
    distance = strip_row - patch_row

    def strip(owner):
        shifted = distance + owner * rows
        own_rows = onehot(shifted == top_row)
        peer_rows = onehot(shifted == peer_row)
        return [dot(own_rows, placed[c][0]) + dot(peer_rows, placed[c][1]) for c in range(2)]

    def direct_copy(mask, c):
        place = mask - 1 if c == 0 else probe_count - 1
        return pltpu.make_async_remote_copy(
            src_ref=direct_out.at[place],
            dst_ref=direct_in.at[place],
            send_sem=direct_sems.at[0, place],
            recv_sem=direct_sems.at[1, place],
            device_id={"probe": flip(probe, mask, probe_count)},
            device_id_type=MESH,
        )

    def pair_copy(place):
        return pltpu.make_async_remote_copy(
            src_ref=pair_out.at[place],
            dst_ref=pair_in.at[place],
            send_sem=pair_sems.at[0, place],
            recv_sem=pair_sems.at[1, place],
            device_id={"probe": flip(probe, 1, probe_count)},
            device_id_type=MESH,
        )

    def sum_copy(place):
        return pltpu.make_async_remote_copy(
            src_ref=sum_out.at[place],
            dst_ref=sum_in.at[place],
            send_sem=sum_sems.at[0, place],
            recv_sem=sum_sems.at[1, place],
            device_id={"probe": flip(probe, 2 * place + 2, probe_count)},
            device_id_type=MESH,
        )

    others = range(probe_count // 2 - 1, 0, -1)
    for other in others:
        mask = 2 * other + 1
        real, imag = strip(flip(probe, mask, probe_count))
        pair_out[other - 1] = imag.astype(BF16)
        pair_copy(other - 1).start()
        direct_out[mask - 1] = real.astype(BF16)
        direct_copy(mask, 0).start()
    for other in others:
        mask = 2 * other
        real, imag = strip(flip(probe, mask, probe_count))
        direct_out[mask - 1] = real.astype(BF16)
        direct_copy(mask, 0).start()
        held[other - 1] = imag
    real, imag = strip(flip(probe, 1, probe_count))
    direct_out[0] = real.astype(BF16)
    direct_out[probe_count - 1] = imag.astype(BF16)
    direct_copy(1, 0).start()
    direct_copy(1, 1).start()
    for other in others:
        pair_copy(other - 1).wait_recv()
        sum_out[other - 1] = (held[other - 1] + pair_in[other - 1].astype(F32)).astype(BF16)
        sum_copy(other - 1).start()
    total = strip(probe)
    for c in range(2):
        out[c, 0] = total[c]
    for mask in range(probe_count - 1, 0, -1):
        direct_copy(mask, 0).wait_recv()
        out[0, 0] += direct_in[mask - 1].astype(F32)
    direct_copy(1, 1).wait_recv()
    out[1, 0] += direct_in[probe_count - 1].astype(F32)
    for other in others:
        sum_copy(other - 1).wait_recv()
        out[1, 0] += sum_in[other - 1].astype(F32)

    corner_copy.wait_send()
    for part in range(CHUNKS):
        grad_copy(part).wait_send()
    for mask in range(1, probe_count):
        direct_copy(mask, 0).wait_send()
    direct_copy(1, 1).wait_send()
    for other in others:
        pair_copy(other - 1).wait_send()
        sum_copy(other - 1).wait_send()

    @pl.when(has_below)
    def _():
        for part in range(CHUNKS):
            hand_copy(part).wait_send()


def per_device(depth_count, probe_count, tile_count, waves, layers, residual, offsets, slot):
    side = waves.shape[-1]
    table = propagator(side)
    rows, columns = OBJ // probe_count, OBJ // tile_count
    others = probe_count // 2 - 1
    vmem = pl.BlockSpec(memory_space=pltpu.VMEM)
    smem = pl.BlockSpec(memory_space=pltpu.SMEM)
    hbm = pl.BlockSpec(memory_space=pltpu.HBM)
    return pl.pallas_call(
        functools.partial(kernel, depth_count, probe_count),
        out_shape=jax.ShapeDtypeStruct((2, 1, rows, columns), F32),
        in_specs=[hbm, hbm, hbm, smem, smem, hbm],
        out_specs=vmem,
        scratch_shapes=[
            pltpu.VMEM(waves.shape, waves.dtype),
            pltpu.VMEM(layers.shape, layers.dtype),
            pltpu.VMEM(residual.shape, residual.dtype),
            pltpu.VMEM(table.shape, BF16),
            pltpu.VMEM((2, side, side), BF16),
            pltpu.VMEM((2, side, side), BF16),
            pltpu.VMEM((side, 2 * side), BF16),
            pltpu.VMEM((2, 2, side, side), BF16),
            pltpu.VMEM((2, 16, side), jnp.int32),
            pltpu.VMEM((probe_count, rows, columns), BF16),
            pltpu.VMEM((probe_count, rows, columns), BF16),
            pltpu.VMEM((others, rows, columns), BF16),
            pltpu.VMEM((others, rows, columns), BF16),
            pltpu.VMEM((others, rows, columns), BF16),
            pltpu.VMEM((others, rows, columns), BF16),
            pltpu.VMEM((others, rows, columns), F32),
            pltpu.SemaphoreType.DMA((4,)),
            pltpu.SemaphoreType.DMA((2, CHUNKS)),
            pltpu.SemaphoreType.DMA((2, CHUNKS)),
            pltpu.SemaphoreType.DMA((2,)),
            pltpu.SemaphoreType.DMA((2, probe_count)),
            pltpu.SemaphoreType.DMA((2, others)),
            pltpu.SemaphoreType.DMA((2, others)),
        ],
        compiler_params=pltpu.CompilerParams(
            collective_id=0, has_side_effects=True, vmem_limit_bytes=32 * 1024 * 1024
        ),
    )(
        *(pltpu.with_memory_space_constraint(x, pltpu.HBM) for x in (waves, layers, residual)),
        offsets.T,
        slot,
        pltpu.with_memory_space_constraint(jnp.asarray(table), pltpu.HBM),
    )


def solution(mesh):
    return jax.shard_map(
        functools.partial(per_device, mesh.shape["depth"], mesh.shape["probe"], mesh.shape["tile"]),
        mesh=mesh,
        in_specs=(
            P("depth", ("groups", "probe", "tile"), None, None, None),
            P("depth", ("groups", "probe", "tile"), None, None, None),
            P(("groups", "probe", "tile"), None, None, None),
            P("groups", None),
            P(("groups", "probe", "tile")),
        ),
        out_specs=P("groups", "depth", "probe", "tile"),
        check_vma=False,
    )
```

```python
import functools

import jax
import jax.numpy as jnp
import ml_dtypes
import numpy as np
from jax import lax
from jax.experimental import pallas as pl
from jax.experimental.pallas import tpu as pltpu
from jax.sharding import PartitionSpec as P

OBJ = 512
CHUNKS = 1
MESH = pl.DeviceIdType.MESH
F32 = jnp.float32
BF16 = jnp.bfloat16


def propagator(side):
    counter = np.arange(side)
    frequency = (counter + side // 2) % side - side // 2
    chirp = np.exp(0.5j * frequency.astype(np.float64) ** 2 / side)
    column = np.fft.ifft(chirp)
    matrix = column[(counter[:, None] - counter[None, :]) % side]
    parts = np.concatenate([matrix.real, matrix.imag], axis=1)
    high = parts.astype(ml_dtypes.bfloat16)
    low = (parts - high.astype(np.float64)).astype(ml_dtypes.bfloat16)
    return np.stack([high, low])


def dot(a, b):
    return jnp.dot(a, b, preferred_element_type=F32)


def split(value):
    high = value.astype(BF16)
    return high, (value - high.astype(F32)).astype(BF16)


def conj_times(layer_real, layer_imag, real, imag):
    return (
        layer_real * real + layer_imag * imag,
        layer_real * imag - layer_imag * real,
    )


def flip(index, mask, count):
    result, bit = 0, 1
    while bit < count:
        result = result + ((index // bit + (mask // bit) % 2) % 2) * bit
        bit *= 2
    return result


def kernel(
    depth_count,
    probe_count,
    waves_hbm,
    layers_hbm,
    residual_hbm,
    offsets,
    slot,
    table_hbm,
    out,
    waves,
    layers,
    residual,
    table,
    hand_out,
    hand_in,
    turned,
    grads,
    corners,
    direct_out,
    direct_in,
    pair_out,
    pair_in,
    sum_out,
    sum_in,
    held,
    load_sems,
    hand_sems,
    grad_sems,
    corner_sems,
    direct_sems,
    pair_sems,
    sum_sems,
):
    side = waves.shape[-1]
    rows, columns = out.shape[2], out.shape[3]
    step = side // CHUNKS
    depth = lax.axis_index("depth")
    probe = lax.axis_index("probe")
    tile = lax.axis_index("tile")
    is_top = depth == depth_count - 1
    has_below = depth > 0

    barrier = pltpu.get_barrier_semaphore()
    for mask in range(1, probe_count):
        pl.semaphore_signal(
            barrier, inc=1, device_id={"probe": flip(probe, mask, probe_count)}, device_id_type=MESH
        )
    pl.semaphore_signal(barrier, inc=1, device_id={"tile": 1 - tile}, device_id_type=MESH)

    @pl.when(depth < depth_count - 1)
    def _():
        pl.semaphore_signal(barrier, inc=1, device_id={"depth": depth + 1}, device_id_type=MESH)

    load_residual = pltpu.make_async_copy(residual_hbm, residual, load_sems.at[0])
    load_layers = pltpu.make_async_copy(layers_hbm, layers, load_sems.at[1])
    load_waves = pltpu.make_async_copy(waves_hbm, waves, load_sems.at[2])
    load_table = pltpu.make_async_copy(table_hbm, table, load_sems.at[3])

    @pl.when(is_top)
    def _():
        load_residual.start()

    if depth_count > 1:

        @pl.when(has_below)
        def _():
            load_layers.start()

        @pl.when(jnp.logical_not(is_top))
        def _():
            load_table.start()

    load_waves.start()

    own_slot = slot[0]
    top_row = offsets[0, own_slot]
    left_column = offsets[1, own_slot]
    corners[0, 0:8, :] = jnp.full((8, side), top_row, jnp.int32)
    corners[0, 8:16, :] = jnp.full((8, side), left_column, jnp.int32)

    @pl.when(has_below)
    def _():
        pl.semaphore_wait(barrier, probe_count + 1)

    @pl.when(jnp.logical_not(has_below))
    def _():
        pl.semaphore_wait(barrier, probe_count)

    corner_copy = pltpu.make_async_remote_copy(
        src_ref=corners.at[0],
        dst_ref=corners.at[1],
        send_sem=corner_sems.at[0],
        recv_sem=corner_sems.at[1],
        device_id={"tile": 1 - tile},
        device_id_type=MESH,
    )
    corner_copy.start()

    def hand_copy(part):
        window = pl.ds(part * step, step)
        return pltpu.make_async_remote_copy(
            src_ref=hand_out.at[:, window, :],
            dst_ref=hand_in.at[:, window, :],
            send_sem=hand_sems.at[0, part],
            recv_sem=hand_sems.at[1, part],
            device_id={"depth": depth - 1},
            device_id_type=MESH,
        )

    def grad_copy(part):
        window = pl.ds(part * step, step)
        return pltpu.make_async_remote_copy(
            src_ref=grads.at[0, :, window, :],
            dst_ref=grads.at[1, :, window, :],
            send_sem=grad_sems.at[0, part],
            recv_sem=grad_sems.at[1, part],
            device_id={"tile": 1 - tile},
            device_id_type=MESH,
        )

    def hand_down(part, real, imag):
        window = pl.ds(part * step, step)
        handed = conj_times(
            layers[0, 0, 0, window, :].astype(F32), layers[0, 0, 1, window, :].astype(F32), real, imag
        )
        hand_out[0, window, :] = handed[0].astype(BF16)
        hand_out[1, window, :] = handed[1].astype(BF16)
        hand_copy(part).start()

    def give_gradient(part, real, imag):
        window = pl.ds(part * step, step)
        gradient = conj_times(
            waves[0, 0, 0, window, :].astype(F32), waves[0, 0, 1, window, :].astype(F32), real, imag
        )
        grads[0, 0, window, :] = gradient[0].astype(BF16)
        grads[0, 1, window, :] = gradient[1].astype(BF16)
        grad_copy(part).start()

    @pl.when(is_top)
    def _():
        load_residual.wait()
        if depth_count > 1:
            load_layers.wait()
            for part in range(CHUNKS):
                window = pl.ds(part * step, step)
                hand_down(part, residual[0, 0, window, :], residual[0, 1, window, :])
        load_waves.wait()
        for part in range(CHUNKS):
            window = pl.ds(part * step, step)
            give_gradient(part, residual[0, 0, window, :], residual[0, 1, window, :])

    if depth_count > 1:

        @pl.when(jnp.logical_not(is_top))
        def _():
            load_table.wait()
            load_waves.wait()
            if depth_count > 2:

                @pl.when(has_below)
                def _():
                    load_layers.wait()

            for part in range(CHUNKS):
                window = pl.ds(part * step, step)
                hand_copy(part).wait_recv()
                real = dot(hand_in[0, window, :], table[0]) + dot(hand_in[0, window, :], table[1])
                imag = dot(hand_in[1, window, :], table[0]) + dot(hand_in[1, window, :], table[1])
                product = real[:, :side] - imag[:, side:], real[:, side:] + imag[:, :side]
                for c in range(2):
                    turned[window, pl.ds(c * side, side)] = product[c].astype(BF16)

            for part in range(CHUNKS):
                window = pl.ds(part * step, step)

                def from_left(index):
                    columns = pl.ds(index * side, side)
                    return (
                        dot(table[0, window, columns], turned[...]) + dot(table[1, window, columns], turned[...])
                    )

                by_real, by_imag = from_left(0), from_left(1)
                real = by_real[:, :side] - by_imag[:, side:]
                imag = by_real[:, side:] + by_imag[:, :side]
                if depth_count > 2:

                    @pl.when(has_below)
                    def _():
                        hand_down(part, real, imag)

                give_gradient(part, real, imag)

    row_index = lax.broadcasted_iota(jnp.int32, (side, columns), 0)
    column_index = lax.broadcasted_iota(jnp.int32, (side, columns), 1) + tile * columns

    def onehot(match):
        return jnp.where(match, 1.0, 0.0).astype(BF16)

    own_columns = onehot(column_index - row_index == left_column)
    placed = [[dot(grads[0, c], own_columns).astype(BF16)] for c in range(2)]

    corner_copy.wait_recv()
    for part in range(CHUNKS):
        grad_copy(part).wait_recv()
    peer_row = corners[1, 0:1, :]
    peer_columns = onehot(column_index - row_index == corners[1, 8:9, 0:columns])
    for c in range(2):
        placed[c].append(dot(grads[1, c], peer_columns).astype(BF16))

    strip_row = lax.broadcasted_iota(jnp.int32, (rows, side), 0)
    patch_row = lax.broadcasted_iota(jnp.int32, (rows, side), 1)
    distance = strip_row - patch_row

    def strip_part(owner, c):
        shifted = distance + owner * rows
        own_rows = onehot(shifted == top_row)
        peer_rows = onehot(shifted == peer_row)
        return dot(own_rows, placed[c][0]) + dot(peer_rows, placed[c][1])

    def strip(owner):
        return [strip_part(owner, c) for c in range(2)]

    def direct_copy(mask, c):
        place = mask - 1 if c == 0 else probe_count - 1
        return pltpu.make_async_remote_copy(
            src_ref=direct_out.at[place],
            dst_ref=direct_in.at[place],
            send_sem=direct_sems.at[0, place],
            recv_sem=direct_sems.at[1, place],
            device_id={"probe": flip(probe, mask, probe_count)},
            device_id_type=MESH,
        )

    def pair_copy(place):
        return pltpu.make_async_remote_copy(
            src_ref=pair_out.at[place],
            dst_ref=pair_in.at[place],
            send_sem=pair_sems.at[0, place],
            recv_sem=pair_sems.at[1, place],
            device_id={"probe": flip(probe, 1, probe_count)},
            device_id_type=MESH,
        )

    def sum_copy(place):
        return pltpu.make_async_remote_copy(
            src_ref=sum_out.at[place],
            dst_ref=sum_in.at[place],
            send_sem=sum_sems.at[0, place],
            recv_sem=sum_sems.at[1, place],
            device_id={"probe": flip(probe, 2 * place + 2, probe_count)},
            device_id_type=MESH,
        )

    others = range(probe_count // 2 - 1, 0, -1)
    for other in others:
        mask = 2 * other + 1
        owner = flip(probe, mask, probe_count)
        pair_out[other - 1] = strip_part(owner, 1).astype(BF16)
        pair_copy(other - 1).start()
        direct_out[mask - 1] = strip_part(owner, 0).astype(BF16)
        direct_copy(mask, 0).start()
    for other in others:
        mask = 2 * other
        real, imag = strip(flip(probe, mask, probe_count))
        direct_out[mask - 1] = real.astype(BF16)
        direct_copy(mask, 0).start()
        held[other - 1] = imag
    real, imag = strip(flip(probe, 1, probe_count))
    direct_out[0] = real.astype(BF16)
    direct_out[probe_count - 1] = imag.astype(BF16)
    direct_copy(1, 0).start()
    direct_copy(1, 1).start()
    for other in others:
        pair_copy(other - 1).wait_recv()
        sum_out[other - 1] = (held[other - 1] + pair_in[other - 1].astype(F32)).astype(BF16)
        sum_copy(other - 1).start()
    total = strip(probe)
    for c in range(2):
        out[c, 0] = total[c]
    for mask in range(probe_count - 1, 0, -1):
        direct_copy(mask, 0).wait_recv()
        out[0, 0] += direct_in[mask - 1].astype(F32)
    direct_copy(1, 1).wait_recv()
    out[1, 0] += direct_in[probe_count - 1].astype(F32)
    for other in others:
        sum_copy(other - 1).wait_recv()
        out[1, 0] += sum_in[other - 1].astype(F32)

    corner_copy.wait_send()
    for part in range(CHUNKS):
        grad_copy(part).wait_send()
    for mask in range(1, probe_count):
        direct_copy(mask, 0).wait_send()
    direct_copy(1, 1).wait_send()
    for other in others:
        pair_copy(other - 1).wait_send()
        sum_copy(other - 1).wait_send()

    @pl.when(has_below)
    def _():
        for part in range(CHUNKS):
            hand_copy(part).wait_send()


def per_device(depth_count, probe_count, tile_count, waves, layers, residual, offsets, slot):
    side = waves.shape[-1]
    table = propagator(side)
    rows, columns = OBJ // probe_count, OBJ // tile_count
    others = probe_count // 2 - 1
    vmem = pl.BlockSpec(memory_space=pltpu.VMEM)
    smem = pl.BlockSpec(memory_space=pltpu.SMEM)
    hbm = pl.BlockSpec(memory_space=pltpu.HBM)
    return pl.pallas_call(
        functools.partial(kernel, depth_count, probe_count),
        out_shape=jax.ShapeDtypeStruct((2, 1, rows, columns), F32),
        in_specs=[hbm, hbm, hbm, smem, smem, hbm],
        out_specs=vmem,
        scratch_shapes=[
            pltpu.VMEM(waves.shape, waves.dtype),
            pltpu.VMEM(layers.shape, layers.dtype),
            pltpu.VMEM(residual.shape, residual.dtype),
            pltpu.VMEM(table.shape, BF16),
            pltpu.VMEM((2, side, side), BF16),
            pltpu.VMEM((2, side, side), BF16),
            pltpu.VMEM((side, 2 * side), BF16),
            pltpu.VMEM((2, 2, side, side), BF16),
            pltpu.VMEM((2, 16, side), jnp.int32),
            pltpu.VMEM((probe_count, rows, columns), BF16),
            pltpu.VMEM((probe_count, rows, columns), BF16),
            pltpu.VMEM((others, rows, columns), BF16),
            pltpu.VMEM((others, rows, columns), BF16),
            pltpu.VMEM((others, rows, columns), BF16),
            pltpu.VMEM((others, rows, columns), BF16),
            pltpu.VMEM((others, rows, columns), F32),
            pltpu.SemaphoreType.DMA((4,)),
            pltpu.SemaphoreType.DMA((2, CHUNKS)),
            pltpu.SemaphoreType.DMA((2, CHUNKS)),
            pltpu.SemaphoreType.DMA((2,)),
            pltpu.SemaphoreType.DMA((2, probe_count)),
            pltpu.SemaphoreType.DMA((2, others)),
            pltpu.SemaphoreType.DMA((2, others)),
        ],
        compiler_params=pltpu.CompilerParams(
            collective_id=0, has_side_effects=True, vmem_limit_bytes=32 * 1024 * 1024
        ),
    )(
        *(pltpu.with_memory_space_constraint(x, pltpu.HBM) for x in (waves, layers, residual)),
        offsets.T,
        slot,
        pltpu.with_memory_space_constraint(jnp.asarray(table), pltpu.HBM),
    )


def solution(mesh):
    return jax.shard_map(
        functools.partial(per_device, mesh.shape["depth"], mesh.shape["probe"], mesh.shape["tile"]),
        mesh=mesh,
        in_specs=(
            P("depth", ("groups", "probe", "tile"), None, None, None),
            P("depth", ("groups", "probe", "tile"), None, None, None),
            P(("groups", "probe", "tile"), None, None, None),
            P("groups", None),
            P(("groups", "probe", "tile")),
        ),
        out_specs=P("groups", "depth", "probe", "tile"),
        check_vma=False,
    )
```
